32 devices in a mesh: kgrp: 4 (over x, core), row: 4 (over z), col: 2 (over y).
Axes of the slice: x: 2, y: 2, z: 4, core: 2. Of those that a mesh axis runs over, the one named last changes fastest.
Arguments:
- occ_orbitals: bfloat16 [8, 1024, 2, 512], P('kgrp', ('row', 'col')), may hold values from -5 to 5
- emp_orbitals: bfloat16 [8, 1024, 2, 512], P('kgrp', ('row', 'col')), may hold values from -5 to 5
- energies: float32 [2, 8, 512], replicated, may hold values from 0.05 to 1.5
- band_order: int32 [2, 8, 512], replicated, may hold values from 0 to 511, each once within a row
- imag_times: float32 [2], replicated, may hold values from 0.3 to 3
- kq_map: int32 [2, 8], replicated, may hold values from 0 to 7, each once within a row
- slot_kpoint: int32 [8], replicated, may hold values from 0 to 7, each once
Outputs:
- suscept: float32 [2, 2, 2, 512, 2, 1024], P(None, None, 'col', 'kgrp', None, 'row')
The draws below stay inside these ranges and needn't reach their ends.
Inputs may be any that keep to these rules, and one draw needn't show every extreme that they name: `kq_map`: each row is a permutation of the k-point ids. `slot_kpoint`: a permutation of the k-point ids. `band_order`: each row over the last dimension is a permutation of the ranks.
All inputs are finite; a program needn't handle non-finite values.
Results may differ from the reference program's by a relative error of at most 0.0003.
Values may be sent and summed in bfloat16 or wider, within the bound.
No kernel may reach another device: no remote copies, remote signals or barrier semaphores. Data moves between devices by JAX's collectives and lax.ppermute only.
A program may use at most 64 MiB of HBM per device.

```python
import math
import jax
import jax.numpy as jnp
from jax import lax

NB = 512
NMU = 1024
NQ = 2
NT = 2
K = 8
N_ROW = 4
N_COL = 2


def block_levels(key, shape, pieces, smallest, largest):
    def one(dim, shards_of):
        heights = jax.random.uniform(jax.random.fold_in(jax.random.fold_in(key, 6), dim), (shards_of,), jnp.float32, smallest / len(pieces), largest / len(pieces))
        return jnp.repeat(jnp.exp(heights), shape[dim] // shards_of).reshape((-1,) + (1,) * (len(shape) - dim - 1))

    factor_of = one(*pieces[0])
    for cut in pieces[1:]:
        factor_of = factor_of * one(*cut)
    return factor_of


def centred(stream_key, shape, spread, bound, split=(), held_as=jnp.bfloat16):
    drawn = spread * jax.random.normal(stream_key, shape, jnp.float32)
    if split:
        drawn = drawn * block_levels(stream_key, shape, split, -0.22, 0.18)
    return jnp.clip(drawn, -bound, bound).astype(held_as)


def setup_inputs(seed: int = 0) -> dict:
    arg_keys = jax.random.split(jax.random.key(seed), 8)
    return {
        "occ_orbitals": centred(arg_keys[0], (K, NMU, 2, NB), 0.35, 5.0, ((0, 4), (1, 8))),
        "emp_orbitals": centred(arg_keys[1], (K, NMU, 2, NB), 0.35, 5.0, ((0, 4), (1, 8))),
        "energies": jnp.clip(jnp.exp(jax.random.uniform(arg_keys[2], (2, K, NB), jnp.float32, math.log(0.05), math.log(1.5))), 0.05, 1.5),
        "band_order": jax.vmap(lambda own: jax.random.permutation(own, NB))(jax.random.split(arg_keys[3], 2 * K)).reshape((2, K, NB)).astype(jnp.int32),
        "imag_times": jnp.clip(jnp.exp(jax.random.uniform(arg_keys[4], (NT,), jnp.float32, math.log(0.3), math.log(3.0))), 0.3, 3.0),
        "kq_map": jax.vmap(lambda own: jax.random.permutation(own, K))(jax.random.split(arg_keys[5], NQ)).reshape((NQ, K)).astype(jnp.int32),
        "slot_kpoint": jax.random.permutation(arg_keys[6], K).astype(jnp.int32),
    }


def band_weights(levels, band_rank, imag_times):
    picked = jnp.take_along_axis(levels, band_rank.astype(jnp.int32), axis=0)
    return jnp.exp(-picked[None, :] * imag_times[:, None])


def green_tile(row_panel, col_panel, weights):
    times_count = weights.shape[0]
    scaled = (row_panel[None] * weights[:, None, None, :]).astype(jnp.bfloat16)
    scaled = scaled.reshape(times_count, row_panel.shape[0], -1)
    turned = jnp.concatenate([-col_panel[:, 1], col_panel[:, 0]], axis=1)
    stacked = jnp.concatenate([col_panel.reshape(col_panel.shape[0], -1), turned], axis=0)
    result = lax.dot_general(stacked, scaled, (((1,), (2,)), ((), ())), preferred_element_type=jnp.float32)
    return result.reshape(2, col_panel.shape[0], times_count, row_panel.shape[0])


def pair_term(held_tile, moved_tile, factor):
    real_part = held_tile[0] * moved_tile[0] + held_tile[1] * moved_tile[1]
    imag_part = held_tile[1] * moved_tile[0] - held_tile[0] * moved_tile[1]
    return factor * jnp.stack([real_part, imag_part])


def reference(occ_orbitals, emp_orbitals, energies, band_order, imag_times, kq_map, slot_kpoint):
    kpoints = occ_orbitals.shape[0]
    positions = jnp.arange(kpoints, dtype=jnp.int32)
    inverse = jnp.zeros((kpoints,), jnp.int32).at[slot_kpoint].set(positions)
    sources = inverse[kq_map[:, slot_kpoint]]
    factor = -1.0 / kpoints

    def advance(suscept, slot_index):
        held_tile = green_tile(occ_orbitals[slot_index], occ_orbitals[slot_index],
                               band_weights(energies[0, slot_index], band_order[0, slot_index], imag_times))
        pair_terms = []
        for transfer in range(NQ):
            source = sources[transfer, slot_index]
            moved_tile = green_tile(emp_orbitals[source], emp_orbitals[source],
                                    band_weights(energies[1, source], band_order[1, source], imag_times))
            pair_terms.append(pair_term(held_tile, moved_tile, factor))
        return suscept + jnp.stack(pair_terms, axis=1), None

    initial = jnp.zeros((2, NQ, NMU, NT, NMU), jnp.float32)
    suscept, unused = lax.scan(advance, initial, positions)
    suscept = suscept.reshape(2, NQ, N_ROW, N_COL, NMU // (N_ROW * N_COL), NT, NMU)
    suscept = jnp.transpose(suscept, (0, 1, 3, 2, 4, 5, 6))
    return suscept.reshape(2, NQ, N_COL, NMU // N_COL, NT, NMU)
```

```python
import functools

import jax
import jax.numpy as jnp
from jax import lax
from jax.experimental import pallas as pl
from jax.experimental.pallas import tpu as pltpu
from jax.sharding import PartitionSpec as P


def table_row(lookup_table, wanted):
    positions = jnp.arange(lookup_table.shape[0], dtype=jnp.int32)
    chosen = positions[:, None] == wanted
    return jnp.sum(jnp.where(chosen, lookup_table, jnp.zeros_like(lookup_table)), axis=0)


def band_weights(levels, band_rank, imag_times):
    picked = jnp.take(levels, band_rank, axis=0)
    return jnp.exp(-picked[None, :] * imag_times[:, None])


def green_tile(row_panel, col_panel, weights):
    times_count = weights.shape[0]
    scaled = (row_panel[None] * weights[:, None, None, :]).astype(jnp.bfloat16)
    scaled = scaled.reshape(times_count, row_panel.shape[0], -1)
    turned = jnp.concatenate([-col_panel[:, 1], col_panel[:, 0]], axis=1)
    stacked = jnp.concatenate([col_panel.reshape(col_panel.shape[0], -1), turned], axis=0)
    result = lax.dot_general(
        stacked, scaled, (((1,), (2,)), ((), ())), preferred_element_type=jnp.float32
    )
    return result.reshape(2, col_panel.shape[0], times_count, row_panel.shape[0])


def pair_term(held_tile, moved_tile, factor):
    real_part = held_tile[0] * moved_tile[0] + held_tile[1] * moved_tile[1]
    imag_part = held_tile[1] * moved_tile[0] - held_tile[0] * moved_tile[1]
    return factor * jnp.stack([real_part, imag_part])


def source_slots(kq_map, slot_kpoint, own_slots):
    positions = jnp.arange(slot_kpoint.shape[0], dtype=jnp.int32)
    own_kpoint = jnp.sum(
        jnp.where(own_slots[:, None] == positions[None, :], slot_kpoint[None, :], 0), axis=1
    )
    target = jnp.sum(
        jnp.where(own_kpoint[None, :, None] == positions[None, None, :], kq_map[:, None, :], 0),
        axis=2,
    )
    return jnp.sum(
        jnp.where(target[:, :, None] == slot_kpoint[None, None, :], positions[None, None, :], 0),
        axis=2,
    )


def summed_over_groups(occ_orbitals, emp_orbitals, energies, band_order, imag_times, kq_map, slot_kpoint):
    groups = lax.axis_size("kgrp")
    per_group = occ_orbitals.shape[0]
    kpoints = groups * per_group
    transfers = kq_map.shape[0]
    factor = -1.0 / kpoints
    own_slots = lax.axis_index("kgrp") * per_group + jnp.arange(per_group, dtype=jnp.int32)
    sources = source_slots(kq_map, slot_kpoint, own_slots)
    flat_sources = sources.reshape(-1)
    initial = jnp.zeros((flat_sources.shape[0],) + emp_orbitals.shape[1:], jnp.float32)
    block_part = lax.all_gather(emp_orbitals, "kgrp", axis=0, tiled=True)
    numbered = block_part.shape[0]
    matches = (flat_sources[:, None] == jnp.arange(numbered, dtype=jnp.int32)[None, :]).astype(
        jnp.bfloat16
    )
    update = jnp.dot(matches, block_part.reshape(numbered, -1), preferred_element_type=jnp.float32)
    fetched = update.reshape(initial.shape).astype(jnp.bfloat16)
    occ_rows, emp_rows = (
        lax.all_gather(occ_orbitals, "col", axis=1, tiled=True),
        lax.all_gather(fetched, "col", axis=1, tiled=True),
    )
    occ_cols, emp_cols = (
        lax.all_gather(occ_orbitals, "row", axis=1, tiled=True),
        lax.all_gather(fetched, "row", axis=1, tiled=True),
    )
    tiles = []
    for position in range(per_group):
        weights = band_weights(
            table_row(energies[0], own_slots[position]),
            table_row(band_order[0], own_slots[position]),
            imag_times,
        )
        tiles.append(green_tile(occ_rows[position], occ_cols[position], weights))

    def transfer_terms(transfer):
        partial_value = None
        for position in range(per_group):
            source = sources[transfer, position]
            weights = band_weights(
                table_row(energies[1], source), table_row(band_order[1], source), imag_times
            )
            moved_index = transfer * per_group + position
            moved_tile = green_tile(emp_rows[moved_index], emp_cols[moved_index], weights)
            addition = pair_term(tiles[position], moved_tile, factor)
            partial_value = addition if partial_value is None else partial_value + addition
        return partial_value

    terms_all = jnp.stack([transfer_terms(transfer) for transfer in range(transfers)], axis=1)
    summed = lax.psum_scatter(terms_all, "kgrp", scatter_dimension=2, tiled=True)
    return summed[:, :, None]


LANES = 128
ANY = pl.BlockSpec(memory_space=pl.ANY)
VMEM = pl.BlockSpec(memory_space=pltpu.VMEM)
SMEM = pl.BlockSpec(memory_space=pltpu.SMEM)
AXES = ("kgrp", "row", "col")


def place():
    group = lax.axis_index("kgrp")
    return lax.div(group, 2), lax.rem(group, 2), lax.axis_index("row"), lax.axis_index("col")


def prep_kernel(levels_ref, rank_ref, times_ref, map_ref, kpoint_ref, weight_ref, pair_ref, slot_of):
    bands = levels_ref.shape[2]
    times = weight_ref.shape[1]
    for kind in range(2):
        for start in range(0, bands, LANES):
            rank = rank_ref[kind, :, start : start + LANES]
            low, high = rank & (LANES - 1), rank // LANES
            picked = jnp.zeros(rank.shape, jnp.float32)
            for piece in range(bands // LANES):
                table = levels_ref[kind, :, piece * LANES : (piece + 1) * LANES]
                found = jnp.take_along_axis(table, low, axis=1)
                picked = jnp.where(high == piece, found, picked)
            for t in range(times):
                value = jnp.exp(-picked * times_ref[t])
                weight_ref[kind, t, :, start : start + LANES] = value
                weight_ref[kind, t, :, bands + start : bands + start + LANES] = value
    transfers, kpoints = map_ref.shape
    per_group = kpoints // lax.axis_size("kgrp")
    group = lax.axis_index("kgrp")

    def relative(slot):
        return (lax.div(slot, per_group) ^ group) * per_group + lax.rem(slot, per_group)

    for slot in range(kpoints):
        slot_of[kpoint_ref[slot]] = slot
    for transfer in range(transfers):
        for slot in range(kpoints):
            source = slot_of[map_ref[transfer, kpoint_ref[slot]]]
            pair_ref[transfer, relative(source)] = relative(jnp.int32(slot))


def choose():
    x, h, z, _ = place()
    half = lax.axis_size("row") // 2
    near = x == lax.div(z, half)
    inner = (z == half - 1) | (z == half)
    owns = h == lax.rem(z, 2)
    first = h == lax.div(z, half)
    far1 = jnp.where(inner, 2, 4)
    far2 = jnp.where(inner, 3, 5)
    keep = jnp.where(near, jnp.where(owns, 0, 1), jnp.where(first, far1, far2))
    send = jnp.where(near, jnp.where(owns, 1, 0), jnp.where(first, far2, far1))
    return keep, send


def pack_kernel(kind, *refs):
    direct, crossed = refs[0:6], refs[6:12]
    keep_ref, send_ref, sems = refs[12:15]
    keep, send = choose()
    slots = keep_ref.shape[1]

    def part(ref):
        return ref if ref.shape[0] == slots else ref.at[pl.ds(kind * slots, slots)]

    for case in range(6):
        for slot, (wanted, target) in enumerate(((send, send_ref), (keep, keep_ref))):

            @pl.when(wanted == case)
            def _():
                pltpu.make_async_copy(part(direct[case]), target.at[0], sems.at[slot, 0]).start()
                pltpu.make_async_copy(part(crossed[case]), target.at[1], sems.at[slot, 1]).start()

    for slot, target in enumerate((send_ref, keep_ref)):
        for side in range(2):
            pltpu.make_async_copy(target.at[side], target.at[side], sems.at[slot, side]).wait()


def pack(kind, direct, crossed, shape):
    return pl.pallas_call(
        functools.partial(pack_kernel, kind),
        out_shape=[jax.ShapeDtypeStruct((2,) + shape, jnp.bfloat16)] * 2,
        in_specs=[ANY] * 12,
        out_specs=[VMEM] * 2,
        scratch_shapes=[pltpu.SemaphoreType.DMA((2, 2))],
        name="pack%d" % kind,
    )(*direct, *crossed)


def load_panels(kind, rows, keep, recv, row_buf, col_buf, sems):
    slots = col_buf.shape[1]
    copies = []
    for k in range(4):
        source = (keep, recv)[k & 1].at[k >> 1]
        group = [pltpu.make_async_copy(source, col_buf.at[k], sems.at[k, 0])]
        for half in range(2):
            part = rows[half * 4 + k].at[pl.ds(kind * slots, slots)]
            group.append(pltpu.make_async_copy(part, row_buf.at[half, k], sems.at[k, 1 + half]))
        for copy in group:
            copy.start()
        copies.append(group)
    return copies


def tile(kind, k, i, half, stacked, row_buf, weight_ref):
    per_group = row_buf.shape[2]
    slot = (lax.axis_index("kgrp") ^ k) * per_group + i
    panel = row_buf[half, k, i].astype(jnp.float32)
    scaled = [
        (panel * weight_ref[kind, t, pl.ds(slot, 1), :]).astype(jnp.bfloat16)
        for t in range(weight_ref.shape[1])
    ]
    return lax.dot_general(
        stacked,
        jnp.concatenate(scaled, axis=0),
        (((1,), (1,)), ((), ())),
        preferred_element_type=jnp.float32,
    )


def stack_columns(columns):
    width = columns.shape[1] // 2
    turned = jnp.concatenate([-columns[:, width:], columns[:, :width]], axis=1)
    return jnp.concatenate([columns, turned], axis=0)


def occ_kernel(*refs):
    rows, keep, recv, weight_ref = refs[:8], refs[8], refs[9], refs[10]
    out_ref, row_buf, col_buf, sems = refs[11:]
    copies = load_panels(0, rows, keep, recv, row_buf, col_buf, sems)
    per_group = col_buf.shape[1]
    for k in range(4):
        for copy in copies[k]:
            copy.wait()
        for i in range(per_group):
            stacked = stack_columns(col_buf[k, i])
            for half in range(2):
                out_ref[k * per_group + i, half] = tile(0, k, i, half, stacked, row_buf, weight_ref)


def emp_kernel(factor, *refs):
    rows, keep, recv, weight_ref, pair_ref, occ_ref = refs[:8], refs[8], refs[9], refs[10], refs[11], refs[12]
    out_ref, row_buf, col_buf, acc, sems = refs[13:]
    copies = load_panels(1, rows, keep, recv, row_buf, col_buf, sems)
    per_group, block = col_buf.shape[1], col_buf.shape[2]
    transfers = pair_ref.shape[0]
    times = weight_ref.shape[1]
    y = lax.axis_index("col")
    for k in range(4):
        for copy in copies[k]:
            copy.wait()
        for i in range(per_group):
            stacked = stack_columns(col_buf[k, i])
            a = k * per_group + i
            for half in range(2):
                moved = tile(1, k, i, half, stacked, row_buf, weight_ref)
                re, im = moved[:block], moved[block:]
                for q in range(transfers):
                    held = pair_ref[q, a]
                    ro = occ_ref[held, half, :block]
                    io = occ_ref[held, half, block:]
                    real = ro * re + io * im
                    imag = io * re - ro * im
                    if a == 0:
                        acc[q, half, 0] = real
                        acc[q, half, 1] = imag
                    elif a < 4 * per_group - 1:
                        acc[q, half, 0] += real
                        acc[q, half, 1] += imag
                    else:
                        start = pl.multiple_of((y ^ half) * block, LANES)
                        for comp, last in enumerate((real, imag)):
                            total = (acc[q, half, comp] + last) * factor
                            for t in range(times):
                                out_ref[comp, q, :, t, pl.ds(start, block)] = total[:, t * block : (t + 1) * block]


def output_stationary(occ_orbitals, emp_orbitals, energies, band_order, imag_times, kq_map, slot_kpoint):
    groups, rows, cols = (lax.axis_size(name) for name in AXES)
    slots, block = occ_orbitals.shape[:2]
    width = occ_orbitals.shape[2] * occ_orbitals.shape[3]
    transfers, times = kq_map.shape[0], imag_times.shape[0]
    kpoints = groups * slots
    half = rows // 2
    top = rows - 1

    def send(array, route):
        pairs = []
        for g in range(groups):
            for z in range(rows):
                for y in range(cols):
                    target = route(g // 2, g % 2, z, y)
                    if target is not None:
                        x2, h2, z2, y2 = target
                        pairs.append(((g * rows + z) * cols + y, ((2 * x2 + h2) * rows + z2) * cols + y2))
        return lax.ppermute(array, AXES, pairs)

    def inner(z):
        return z in (half - 1, half)

    def near(x, z):
        return x == z // half

    def swap(x, h, z, y):
        return x, h, z ^ 1, y

    def swap_main(x, h, z, y):
        return None if inner(z) and near(x, z) else (x, h, z ^ 1, y)

    def swap_late(x, h, z, y):
        return (x, h, z ^ 1, y) if inner(z) and near(x, z) else None

    def middle(x, h, z, y):
        return (x, h, top - z, y) if inner(z) else None

    def outward(x, h, z, y):
        return (x, h, z ^ 1, y) if inner(z) else None

    def flip_x(x, h, z, y):
        return 1 - x, h, z, y

    def to_near(x, h, z, y):
        return None if near(x, z) else (1 - x, h, z, y)

    def to_far_inner(x, h, z, y):
        return (1 - x, h, z, y) if near(x, z) and inner(z) else None

    def to_far_outer(x, h, z, y):
        return (1 - x, h, z, y) if near(x, z) and not inner(z) else None

    def flip_y(x, h, z, y):
        return x, h, z, 1 - y

    def flip_core(x, h, z, y):
        return x, 1 - h, z, y

    kinds = [occ_orbitals.reshape(slots, block, width), emp_orbitals.reshape(slots, block, width)]
    both = jnp.concatenate(kinds, axis=0)

    weights, pairs = pl.pallas_call(
        prep_kernel,
        out_shape=[
            jax.ShapeDtypeStruct((2, times, kpoints, width), jnp.float32),
            jax.ShapeDtypeStruct((transfers, kpoints), jnp.int32),
        ],
        in_specs=[VMEM, VMEM, SMEM, SMEM, SMEM],
        out_specs=[VMEM, SMEM],
        scratch_shapes=[pltpu.SMEM((kpoints,), jnp.int32)],
        name="prep",
    )(energies, band_order, imag_times, kq_map, slot_kpoint)

    s1, b, d, e, f = [None] * 2, [None] * 2, [None] * 2, [None] * 2, [None] * 2
    s1x, bx, dx, ex, fx = [None] * 2, [None] * 2, [None] * 2, [None] * 2, [None] * 2
    for kind in range(2):
        s1[kind] = send(kinds[kind], swap)
        b[kind] = send(kinds[kind], middle)
    crossed = send(both, flip_x)
    turned = send(both, flip_y)
    sibling = send(both, flip_core)
    for kind in range(2):
        e[kind] = send(b[kind], outward)
        d[kind] = send(s1[kind], middle)
    turned_crossed = send(crossed, flip_y)
    crossed_sibling = send(crossed, flip_core)
    turned_sibling = send(turned, flip_core)
    for kind in range(2):
        s1x[kind] = send(s1[kind], to_near)
        bx[kind] = send(b[kind], to_far_inner)
        f[kind] = send(d[kind], outward)
        ex[kind] = send(e[kind], to_far_outer)
        dx[kind] = send(d[kind], to_far_inner)
    turned_crossed_sibling = send(turned_crossed, flip_core)
    for kind in range(2):
        fx[kind] = send(f[kind], to_far_outer)

    row_panels = [
        both, sibling, crossed, crossed_sibling,
        turned, turned_sibling, turned_crossed, turned_crossed_sibling,
    ]
    held, given = [], []
    for kind in range(2):
        keep, give = pack(
            kind,
            [both, s1[kind], b[kind], d[kind], e[kind], f[kind]],
            [crossed, s1x[kind], bx[kind], dx[kind], ex[kind], fx[kind]],
            (slots, block, width),
        )
        held.append(keep)
        given.append(send(give, flip_core))

    panel_scratch = [
        pltpu.VMEM((2, 4, slots, block, width), jnp.bfloat16),
        pltpu.VMEM((4, slots, block, width), jnp.bfloat16),
    ]
    tiles = pl.pallas_call(
        occ_kernel,
        out_shape=jax.ShapeDtypeStruct((kpoints, 2, 2 * block, times * block), jnp.float32),
        in_specs=[ANY] * 10 + [VMEM],
        out_specs=VMEM,
        scratch_shapes=panel_scratch + [pltpu.SemaphoreType.DMA((4, 3))],
        name="occ_tiles",
    )(*row_panels, held[0], given[0], weights)
    result = pl.pallas_call(
        functools.partial(emp_kernel, -1.0 / kpoints),
        out_shape=jax.ShapeDtypeStruct((2, transfers, block, times, cols * block), jnp.float32),
        in_specs=[ANY] * 10 + [VMEM, SMEM, VMEM],
        out_specs=VMEM,
        scratch_shapes=panel_scratch
        + [
            pltpu.VMEM((transfers, 2, 2, block, times * block), jnp.float32),
            pltpu.SemaphoreType.DMA((4, 3)),
        ],
        name="emp_tiles",
    )(*row_panels, held[1], given[1], weights, pairs, tiles)
    return result[:, :, None]


def shards(*arguments):
    groups, rows, cols = (lax.axis_size(name) for name in AXES)
    if groups == rows == 2 * cols == 4:
        return output_stationary(*arguments)
    return summed_over_groups(*arguments)


def solution(mesh):
    in_specs = (
        P("kgrp", ("row", "col"), None, None),
        P("kgrp", ("row", "col"), None, None),
        P(),
        P(),
        P(),
        P(),
        P(),
    )
    out_specs = P(None, None, "col", "kgrp", None, "row")
    return jax.shard_map(shards, mesh=mesh, in_specs=in_specs, out_specs=out_specs, check_vma=False)
```

```python
import functools

import jax
import jax.numpy as jnp
from jax import lax
from jax.experimental import pallas as pl
from jax.experimental.pallas import tpu as pltpu
from jax.sharding import PartitionSpec as P


def table_row(lookup_table, wanted):
    positions = jnp.arange(lookup_table.shape[0], dtype=jnp.int32)
    chosen = positions[:, None] == wanted
    return jnp.sum(jnp.where(chosen, lookup_table, jnp.zeros_like(lookup_table)), axis=0)


def band_weights(levels, band_rank, imag_times):
    picked = jnp.take(levels, band_rank, axis=0)
    return jnp.exp(-picked[None, :] * imag_times[:, None])


def green_tile(row_panel, col_panel, weights):
    times_count = weights.shape[0]
    scaled = (row_panel[None] * weights[:, None, None, :]).astype(jnp.bfloat16)
    scaled = scaled.reshape(times_count, row_panel.shape[0], -1)
    turned = jnp.concatenate([-col_panel[:, 1], col_panel[:, 0]], axis=1)
    stacked = jnp.concatenate([col_panel.reshape(col_panel.shape[0], -1), turned], axis=0)
    result = lax.dot_general(
        stacked, scaled, (((1,), (2,)), ((), ())), preferred_element_type=jnp.float32
    )
    return result.reshape(2, col_panel.shape[0], times_count, row_panel.shape[0])


def pair_term(held_tile, moved_tile, factor):
    real_part = held_tile[0] * moved_tile[0] + held_tile[1] * moved_tile[1]
    imag_part = held_tile[1] * moved_tile[0] - held_tile[0] * moved_tile[1]
    return factor * jnp.stack([real_part, imag_part])


def source_slots(kq_map, slot_kpoint, own_slots):
    positions = jnp.arange(slot_kpoint.shape[0], dtype=jnp.int32)
    own_kpoint = jnp.sum(
        jnp.where(own_slots[:, None] == positions[None, :], slot_kpoint[None, :], 0), axis=1
    )
    target = jnp.sum(
        jnp.where(own_kpoint[None, :, None] == positions[None, None, :], kq_map[:, None, :], 0),
        axis=2,
    )
    return jnp.sum(
        jnp.where(target[:, :, None] == slot_kpoint[None, None, :], positions[None, None, :], 0),
        axis=2,
    )


def summed_over_groups(occ_orbitals, emp_orbitals, energies, band_order, imag_times, kq_map, slot_kpoint):
    groups = lax.axis_size("kgrp")
    per_group = occ_orbitals.shape[0]
    kpoints = groups * per_group
    transfers = kq_map.shape[0]
    factor = -1.0 / kpoints
    own_slots = lax.axis_index("kgrp") * per_group + jnp.arange(per_group, dtype=jnp.int32)
    sources = source_slots(kq_map, slot_kpoint, own_slots)
    flat_sources = sources.reshape(-1)
    initial = jnp.zeros((flat_sources.shape[0],) + emp_orbitals.shape[1:], jnp.float32)
    block_part = lax.all_gather(emp_orbitals, "kgrp", axis=0, tiled=True)
    numbered = block_part.shape[0]
    matches = (flat_sources[:, None] == jnp.arange(numbered, dtype=jnp.int32)[None, :]).astype(
        jnp.bfloat16
    )
    update = jnp.dot(matches, block_part.reshape(numbered, -1), preferred_element_type=jnp.float32)
    fetched = update.reshape(initial.shape).astype(jnp.bfloat16)
    occ_rows, emp_rows = (
        lax.all_gather(occ_orbitals, "col", axis=1, tiled=True),
        lax.all_gather(fetched, "col", axis=1, tiled=True),
    )
    occ_cols, emp_cols = (
        lax.all_gather(occ_orbitals, "row", axis=1, tiled=True),
        lax.all_gather(fetched, "row", axis=1, tiled=True),
    )
    tiles = []
    for position in range(per_group):
        weights = band_weights(
            table_row(energies[0], own_slots[position]),
            table_row(band_order[0], own_slots[position]),
            imag_times,
        )
        tiles.append(green_tile(occ_rows[position], occ_cols[position], weights))

    def transfer_terms(transfer):
        partial_value = None
        for position in range(per_group):
            source = sources[transfer, position]
            weights = band_weights(
                table_row(energies[1], source), table_row(band_order[1], source), imag_times
            )
            moved_index = transfer * per_group + position
            moved_tile = green_tile(emp_rows[moved_index], emp_cols[moved_index], weights)
            addition = pair_term(tiles[position], moved_tile, factor)
            partial_value = addition if partial_value is None else partial_value + addition
        return partial_value

    terms_all = jnp.stack([transfer_terms(transfer) for transfer in range(transfers)], axis=1)
    summed = lax.psum_scatter(terms_all, "kgrp", scatter_dimension=2, tiled=True)
    return summed[:, :, None]


LANES = 128
HBM = pl.BlockSpec(memory_space=pltpu.HBM)
VMEM = pl.BlockSpec(memory_space=pltpu.VMEM)
SMEM = pl.BlockSpec(memory_space=pltpu.SMEM)
LIMIT = pltpu.CompilerParams(vmem_limit_bytes=24 * 2**20)
AXES = ("kgrp", "row", "col")


def place():
    group = lax.axis_index("kgrp")
    return lax.div(group, 2), lax.rem(group, 2), lax.axis_index("row"), lax.axis_index("col")


def prep_kernel(levels_ref, rank_ref, times_ref, map_ref, kpoint_ref, weight_ref, pair_ref, slot_of):
    bands = levels_ref.shape[2]
    times = weight_ref.shape[1]
    for kind in range(2):
        for start in range(0, bands, LANES):
            rank = rank_ref[kind, :, start : start + LANES]
            low, high = rank & (LANES - 1), rank // LANES
            picked = jnp.zeros(rank.shape, jnp.float32)
            for piece in range(bands // LANES):
                table = levels_ref[kind, :, piece * LANES : (piece + 1) * LANES]
                found = jnp.take_along_axis(table, low, axis=1)
                picked = jnp.where(high == piece, found, picked)
            for t in range(times):
                value = jnp.exp(-picked * times_ref[t])
                weight_ref[kind, t, :, start : start + LANES] = value
                weight_ref[kind, t, :, bands + start : bands + start + LANES] = value
    transfers, kpoints = map_ref.shape
    per_group = kpoints // lax.axis_size("kgrp")
    group = lax.axis_index("kgrp")

    def relative(slot):
        return (lax.div(slot, per_group) ^ group) * per_group + lax.rem(slot, per_group)

    for slot in range(kpoints):
        slot_of[kpoint_ref[slot]] = slot
    for transfer in range(transfers):
        for slot in range(kpoints):
            source = slot_of[map_ref[transfer, kpoint_ref[slot]]]
            pair_ref[transfer, relative(source)] = relative(jnp.int32(slot))


def flatten_occ_kernel(occ_ref, occ_out):
    for slot in range(occ_out.shape[0]):
        occ_out[slot] = occ_ref[slot].reshape(occ_out.shape[1:])


def flatten_emp_kernel(emp_ref, occ_flat_ref, emp_out, both_out):
    slots = emp_out.shape[0]
    for slot in range(slots):
        panel = emp_ref[slot].reshape(emp_out.shape[1:])
        emp_out[slot] = panel
        both_out[slot] = occ_flat_ref[slot]
        both_out[slots + slot] = panel


def choose():
    x, h, z, _ = place()
    half = lax.axis_size("row") // 2
    near = x == lax.div(z, half)
    inner = (z == half - 1) | (z == half)
    owns = h == lax.rem(z, 2)
    first = h == lax.div(z, half)
    swapped = jnp.where(inner, 1, 2)
    far1 = jnp.where(inner, 3, 5)
    far2 = jnp.where(inner, 4, 6)
    keep = jnp.where(near, jnp.where(owns, 0, swapped), jnp.where(first, far1, far2))
    send = jnp.where(near, jnp.where(owns, swapped, 0), jnp.where(first, far2, far1))
    return keep, send


def part(ref, kind, slots):
    return ref if ref.shape[0] == slots else ref.at[pl.ds(kind * slots, slots)]


def pack_kernel(kind, cases, *refs):
    direct, crossed = refs[:cases], refs[cases : 2 * cases]
    send_ref, sems = refs[2 * cases :]
    _, send = choose()
    slots = send_ref.shape[1]
    for case in range(cases):

        @pl.when(send == case)
        def _():
            for side, source in enumerate((direct[case], crossed[case])):
                pltpu.make_async_copy(part(source, kind, slots), send_ref.at[side], sems.at[side]).start()

    for side in range(2):
        pltpu.make_async_copy(send_ref.at[side], send_ref.at[side], sems.at[side]).wait()


def pack(kind, direct, crossed, shape):
    return pl.pallas_call(
        functools.partial(pack_kernel, kind, len(direct)),
        out_shape=jax.ShapeDtypeStruct((2,) + shape, jnp.bfloat16),
        in_specs=[HBM] * (2 * len(direct)),
        out_specs=VMEM,
        scratch_shapes=[pltpu.SemaphoreType.DMA((2,))],
        compiler_params=LIMIT,
    )(*direct, *crossed)


def load_panels(kind, groups, rows, direct, crossed, recv, last, row_buf, col_buf, sems):
    slots = col_buf.shape[1]
    keep, _ = choose()

    def fetch(source, k):
        pltpu.make_async_copy(part(source, kind, slots), col_buf.at[k], sems.at[k, 0]).start()

    for k in groups:
        if k & 1:
            inside = recv.at[k >> 1]
            if last is None or k == 1:
                fetch(inside, k)
            else:
                pl.when(keep == 6)(functools.partial(fetch, last, k))
                pl.when(keep != 6)(functools.partial(fetch, inside, k))
        else:
            for case, source in enumerate((direct, crossed)[k >> 1]):
                pl.when(keep == case)(functools.partial(fetch, source, k))
        for half in range(2):
            panel = part(rows[half * 4 + k], kind, slots)
            pltpu.make_async_copy(panel, row_buf.at[half, k], sems.at[k, 1 + half]).start()

    def wait(k):
        for index, target in enumerate((col_buf.at[k], row_buf.at[0, k], row_buf.at[1, k])):
            pltpu.make_async_copy(target, target, sems.at[k, index]).wait()

    return wait


def tile(kind, k, i, half, stacked, row_buf, weight_ref):
    per_group = row_buf.shape[2]
    slot = (lax.axis_index("kgrp") ^ k) * per_group + i
    panel = row_buf[half, k, i].astype(jnp.float32)
    scaled = [
        (panel * weight_ref[kind, t, pl.ds(slot, 1), :]).astype(jnp.bfloat16)
        for t in range(weight_ref.shape[1])
    ]
    return lax.dot_general(
        stacked,
        jnp.concatenate(scaled, axis=0),
        (((1,), (1,)), ((), ())),
        preferred_element_type=jnp.float32,
    )


def stack_columns(columns):
    width = columns.shape[1] // 2
    turned = jnp.concatenate([-columns[:, width:], columns[:, :width]], axis=1)
    return jnp.concatenate([columns, turned], axis=0)


def occ_kernel(cases, *refs):
    rows, direct, crossed = refs[:8], refs[8 : 8 + cases], refs[8 + cases : 8 + 2 * cases]
    recv, weight_ref, out_ref, row_buf, col_buf, sems = refs[8 + 2 * cases :]
    wait = load_panels(0, range(4), rows, direct, crossed, recv, None, row_buf, col_buf, sems)
    per_group = col_buf.shape[1]
    for k in range(4):
        wait(k)
        for i in range(per_group):
            stacked = stack_columns(col_buf[k, i])
            for half in range(2):
                out_ref[k * per_group + i, half] = tile(0, k, i, half, stacked, row_buf, weight_ref)


def emp_direct_kernel(cases, *refs):
    rows, direct = refs[:8], refs[8 : 8 + cases]
    recv, weight_ref, out_ref, row_buf, col_buf, sems = refs[8 + cases :]
    wait = load_panels(1, (0, 1), rows, direct, None, recv, None, row_buf, col_buf, sems)
    per_group = col_buf.shape[1]
    for k in (0, 1):
        wait(k)
        for i in range(per_group):
            stacked = stack_columns(col_buf[k, i])
            for half in range(2):
                out_ref[k * per_group + i, half] = tile(1, k, i, half, stacked, row_buf, weight_ref)


STRIP = 16


def closing_kernel(factor, cases, *refs):
    rows, crossed = refs[:8], refs[8 : 8 + cases]
    recv, last, weight_ref, pair_ref, occ_ref, direct_ref, out_ref, row_buf, col_buf, moved, sems = refs[8 + cases :]
    wait = load_panels(1, (2, 3), rows, None, crossed, recv, last, row_buf, col_buf, sems)
    per_group, block = col_buf.shape[1], col_buf.shape[2]
    split = 2 * per_group
    transfers = pair_ref.shape[0]
    times = weight_ref.shape[1]
    y = lax.axis_index("col")
    for k in (2, 3):
        wait(k)
        for i in range(per_group):
            stacked = stack_columns(col_buf[k, i])
            for half in range(2):
                moved[k * per_group + i - split, half] = tile(1, k, i, half, stacked, row_buf, weight_ref)
    held = [[pair_ref[q, a] for a in range(2 * split)] for q in range(transfers)]
    for half in range(2):
        start = pl.multiple_of((y ^ half) * block, LANES)

        def strip(index, carry):
            real_rows = pl.ds(pl.multiple_of(index * STRIP, STRIP), STRIP)
            imag_rows = pl.ds(pl.multiple_of(index * STRIP + block, STRIP), STRIP)
            sums = [[None, None] for _ in range(transfers)]
            for a in range(2 * split):
                source = direct_ref if a < split else moved
                re = source[a % split, half, real_rows, :]
                im = source[a % split, half, imag_rows, :]
                for q in range(transfers):
                    ro = occ_ref[held[q][a], half, real_rows, :]
                    io = occ_ref[held[q][a], half, imag_rows, :]
                    for comp, piece in enumerate((ro * re + io * im, io * re - ro * im)):
                        sums[q][comp] = piece if a == 0 else sums[q][comp] + piece
            for q in range(transfers):
                for comp in range(2):
                    total = sums[q][comp] * factor
                    for t in range(times):
                        out_ref[comp, q, real_rows, t, pl.ds(start, block)] = total[:, t * block : (t + 1) * block]
            return carry

        lax.fori_loop(0, block // STRIP, strip, 0)


def output_stationary(occ_orbitals, emp_orbitals, energies, band_order, imag_times, kq_map, slot_kpoint):
    groups, rows, cols = (lax.axis_size(name) for name in AXES)
    slots, block = occ_orbitals.shape[:2]
    width = occ_orbitals.shape[2] * occ_orbitals.shape[3]
    transfers, times = kq_map.shape[0], imag_times.shape[0]
    kpoints = groups * slots
    half = rows // 2
    top = rows - 1

    def send(array, route):
        pairs = []
        for g in range(groups):
            for z in range(rows):
                for y in range(cols):
                    target = route(g // 2, g % 2, z, y)
                    if target is not None:
                        x2, h2, z2, y2 = target
                        pairs.append(((g * rows + z) * cols + y, ((2 * x2 + h2) * rows + z2) * cols + y2))
        return lax.ppermute(array, AXES, pairs)

    def inner(z):
        return z in (half - 1, half)

    def near(x, z):
        return x == z // half

    def swap(x, h, z, y):
        return x, h, z ^ 1, y

    def swap_main(x, h, z, y):
        return None if inner(z) and near(x, z) else (x, h, z ^ 1, y)

    def swap_late(x, h, z, y):
        return (x, h, z ^ 1, y) if inner(z) and near(x, z) else None

    def middle(x, h, z, y):
        return (x, h, top - z, y) if inner(z) else None

    def outward_near(x, h, z, y):
        return (x, h, z ^ 1, y) if inner(z) and near(x, z) else None

    def outward_far(x, h, z, y):
        return (x, h, z ^ 1, y) if inner(z) and not near(x, z) else None

    def flip_x(x, h, z, y):
        return 1 - x, h, z, y

    def middle_or_to_near(x, h, z, y):
        if inner(z):
            return x, h, top - z, y
        return None if near(x, z) else (1 - x, h, z, y)

    def from_near(x, h, z, y):
        if not near(x, z):
            return None
        return (x, h, top - z, y) if inner(z) else (x, h, z ^ 1, y)

    def to_far_or_outward(x, h, z, y):
        if not inner(z):
            return None
        return (1 - x, h, z, y) if near(x, z) else (x, h, z ^ 1, y)

    def to_far_outer(x, h, z, y):
        return (1 - x, h, z, y) if near(x, z) and not inner(z) else None

    def flip_y(x, h, z, y):
        return x, h, z, 1 - y

    def flip_core(x, h, z, y):
        return x, 1 - h, z, y

    flat = jax.ShapeDtypeStruct((slots, block, width), jnp.bfloat16)
    occ_flat = pl.pallas_call(
        flatten_occ_kernel,
        out_shape=flat,
        in_specs=[VMEM],
        out_specs=VMEM,
        compiler_params=LIMIT,
        name="flatten_occ",
    )(occ_orbitals)
    emp_flat, both = pl.pallas_call(
        flatten_emp_kernel,
        out_shape=[flat, jax.ShapeDtypeStruct((2 * slots, block, width), jnp.bfloat16)],
        in_specs=[VMEM] * 2,
        out_specs=[VMEM] * 2,
        compiler_params=LIMIT,
        name="flatten_emp",
    )(emp_orbitals, occ_flat)
    kinds = [occ_flat, emp_flat]

    prepare = pl.pallas_call(
        prep_kernel,
        out_shape=[
            jax.ShapeDtypeStruct((2, times, kpoints, width), jnp.float32),
            jax.ShapeDtypeStruct((transfers, kpoints), jnp.int32),
        ],
        in_specs=[VMEM, VMEM, SMEM, SMEM, SMEM],
        out_specs=[VMEM, SMEM],
        scratch_shapes=[pltpu.SMEM((kpoints,), jnp.int32)],
        compiler_params=LIMIT,
        name="prep",
    )
    weights, pairs = prepare(energies, band_order, imag_times, kq_map, slot_kpoint)

    s1 = [send(kinds[0], swap), send(kinds[1], swap_main)]
    late = send(kinds[1], swap_late)
    b = [send(kinds[i], middle) for i in range(2)]
    crossed = send(both, flip_x)
    turned = send(both, flip_y)
    sibling = send(both, flip_core)
    d = [send(s1[i], middle_or_to_near) for i in range(2)]
    en = [send(b[i], outward_near) for i in range(2)]
    e = [send(b[i], outward_far) for i in range(2)]
    bx = send(crossed, from_near)
    turned_crossed = send(crossed, flip_y)
    crossed_sibling = send(crossed, flip_core)
    turned_sibling = send(turned, flip_core)
    turned_crossed_sibling = send(turned_crossed, flip_core)
    ex = [send(en[i], to_far_outer) for i in range(2)]
    fn = [send(d[i], outward_near) for i in range(2)]
    f = [send(d[i], to_far_or_outward) for i in range(2)]
    fx = [send(fn[i], to_far_outer) for i in range(2)]
    last = send(fx[1], flip_core)
    row_panels, direct, across, given = [], [], [], []
    for kind in range(2):
        row_panels.append([
            kinds[kind], sibling, crossed, crossed_sibling,
            turned, turned_sibling, turned_crossed, turned_crossed_sibling,
        ])
        swapped = late if kind else s1[0]
        direct.append([kinds[kind], s1[kind], swapped, b[kind], d[kind], e[kind], f[kind]])
        across.append([crossed, bx, d[kind], bx, f[kind], ex[kind], fx[kind]])
        ready = across[kind][:-1] + [ex[1] if kind else fx[0]]
        give = pack(kind, direct[kind], ready, (slots, block, width))
        given.append(send(give, flip_core))

    panel_scratch = [
        pltpu.VMEM((2, 4, slots, block, width), jnp.bfloat16),
        pltpu.VMEM((4, slots, block, width), jnp.bfloat16),
    ]
    cases = len(direct[0])
    occ_tiles = pl.pallas_call(
        functools.partial(occ_kernel, cases),
        out_shape=jax.ShapeDtypeStruct((kpoints, 2, 2 * block, times * block), jnp.float32),
        in_specs=[HBM] * (9 + 2 * cases) + [VMEM],
        out_specs=VMEM,
        scratch_shapes=panel_scratch + [pltpu.SemaphoreType.DMA((4, 3))],
        compiler_params=LIMIT,
        name="occ_tiles",
    )
    tiles = occ_tiles(*row_panels[0], *direct[0], *across[0], given[0], weights)
    half_tiles = (kpoints // 2, 2, 2 * block, times * block)
    emp_direct = pl.pallas_call(
        functools.partial(emp_direct_kernel, cases),
        out_shape=jax.ShapeDtypeStruct(half_tiles, jnp.float32),
        in_specs=[HBM] * (9 + cases) + [VMEM],
        out_specs=VMEM,
        scratch_shapes=panel_scratch + [pltpu.SemaphoreType.DMA((4, 3))],
        compiler_params=LIMIT,
        name="emp_direct",
    )
    direct_tiles = emp_direct(*row_panels[1], *direct[1], given[1], weights)
    result = pl.pallas_call(
        functools.partial(closing_kernel, -1.0 / kpoints, cases),
        out_shape=jax.ShapeDtypeStruct((2, transfers, block, times, cols * block), jnp.float32),
        in_specs=[HBM] * (10 + cases) + [VMEM, SMEM, VMEM, VMEM],
        out_specs=VMEM,
        scratch_shapes=panel_scratch + [pltpu.VMEM(half_tiles, jnp.float32), pltpu.SemaphoreType.DMA((4, 3))],
        compiler_params=LIMIT,
        name="closing",
    )(*row_panels[1], *across[1], given[1], last, weights, pairs, tiles, direct_tiles)
    return result[:, :, None]


def staged(*arguments):
    return output_stationary(*arguments)


def solution(mesh):
    in_specs = (
        P("kgrp", ("row", "col"), None, None),
        P("kgrp", ("row", "col"), None, None),
        P(),
        P(),
        P(),
        P(),
        P(),
    )
    out_specs = P(None, None, "col", "kgrp", None, "row")
    groups, rows, cols = (mesh.shape[name] for name in AXES)
    line = groups == rows == 2 * cols == 4
    body = staged if line else summed_over_groups
    return jax.shard_map(body, mesh=mesh, in_specs=in_specs, out_specs=out_specs, check_vma=False)
```

```python
import functools

import jax
import jax.numpy as jnp
from jax import lax
from jax.experimental import pallas as pl
from jax.experimental.pallas import tpu as pltpu
from jax.sharding import PartitionSpec as P


def table_row(lookup_table, wanted):
    positions = jnp.arange(lookup_table.shape[0], dtype=jnp.int32)
    chosen = positions[:, None] == wanted
    return jnp.sum(jnp.where(chosen, lookup_table, jnp.zeros_like(lookup_table)), axis=0)


def band_weights(levels, band_rank, imag_times):
    picked = jnp.take(levels, band_rank, axis=0)
    return jnp.exp(-picked[None, :] * imag_times[:, None])


def green_tile(row_panel, col_panel, weights):
    times_count = weights.shape[0]
    scaled = (row_panel[None] * weights[:, None, None, :]).astype(jnp.bfloat16)
    scaled = scaled.reshape(times_count, row_panel.shape[0], -1)
    turned = jnp.concatenate([-col_panel[:, 1], col_panel[:, 0]], axis=1)
    stacked = jnp.concatenate([col_panel.reshape(col_panel.shape[0], -1), turned], axis=0)
    result = lax.dot_general(
        stacked, scaled, (((1,), (2,)), ((), ())), preferred_element_type=jnp.float32
    )
    return result.reshape(2, col_panel.shape[0], times_count, row_panel.shape[0])


def pair_term(held_tile, moved_tile, factor):
    real_part = held_tile[0] * moved_tile[0] + held_tile[1] * moved_tile[1]
    imag_part = held_tile[1] * moved_tile[0] - held_tile[0] * moved_tile[1]
    return factor * jnp.stack([real_part, imag_part])


def source_slots(kq_map, slot_kpoint, own_slots):
    positions = jnp.arange(slot_kpoint.shape[0], dtype=jnp.int32)
    own_kpoint = jnp.sum(
        jnp.where(own_slots[:, None] == positions[None, :], slot_kpoint[None, :], 0), axis=1
    )
    target = jnp.sum(
        jnp.where(own_kpoint[None, :, None] == positions[None, None, :], kq_map[:, None, :], 0),
        axis=2,
    )
    return jnp.sum(
        jnp.where(target[:, :, None] == slot_kpoint[None, None, :], positions[None, None, :], 0),
        axis=2,
    )


def summed_over_groups(occ_orbitals, emp_orbitals, energies, band_order, imag_times, kq_map, slot_kpoint):
    groups = lax.axis_size("kgrp")
    per_group = occ_orbitals.shape[0]
    kpoints = groups * per_group
    transfers = kq_map.shape[0]
    factor = -1.0 / kpoints
    own_slots = lax.axis_index("kgrp") * per_group + jnp.arange(per_group, dtype=jnp.int32)
    sources = source_slots(kq_map, slot_kpoint, own_slots)
    flat_sources = sources.reshape(-1)
    initial = jnp.zeros((flat_sources.shape[0],) + emp_orbitals.shape[1:], jnp.float32)
    block_part = lax.all_gather(emp_orbitals, "kgrp", axis=0, tiled=True)
    numbered = block_part.shape[0]
    matches = (flat_sources[:, None] == jnp.arange(numbered, dtype=jnp.int32)[None, :]).astype(
        jnp.bfloat16
    )
    update = jnp.dot(matches, block_part.reshape(numbered, -1), preferred_element_type=jnp.float32)
    fetched = update.reshape(initial.shape).astype(jnp.bfloat16)
    occ_rows, emp_rows = (
        lax.all_gather(occ_orbitals, "col", axis=1, tiled=True),
        lax.all_gather(fetched, "col", axis=1, tiled=True),
    )
    occ_cols, emp_cols = (
        lax.all_gather(occ_orbitals, "row", axis=1, tiled=True),
        lax.all_gather(fetched, "row", axis=1, tiled=True),
    )
    tiles = []
    for position in range(per_group):
        weights = band_weights(
            table_row(energies[0], own_slots[position]),
            table_row(band_order[0], own_slots[position]),
            imag_times,
        )
        tiles.append(green_tile(occ_rows[position], occ_cols[position], weights))

    def transfer_terms(transfer):
        partial_value = None
        for position in range(per_group):
            source = sources[transfer, position]
            weights = band_weights(
                table_row(energies[1], source), table_row(band_order[1], source), imag_times
            )
            moved_index = transfer * per_group + position
            moved_tile = green_tile(emp_rows[moved_index], emp_cols[moved_index], weights)
            addition = pair_term(tiles[position], moved_tile, factor)
            partial_value = addition if partial_value is None else partial_value + addition
        return partial_value

    terms_all = jnp.stack([transfer_terms(transfer) for transfer in range(transfers)], axis=1)
    summed = lax.psum_scatter(terms_all, "kgrp", scatter_dimension=2, tiled=True)
    return summed[:, :, None]


LANES = 128
HBM = pl.BlockSpec(memory_space=pltpu.HBM)
VMEM = pl.BlockSpec(memory_space=pltpu.VMEM)
SMEM = pl.BlockSpec(memory_space=pltpu.SMEM)
LIMIT = pltpu.CompilerParams(vmem_limit_bytes=24 * 2**20)
AXES = ("kgrp", "row", "col")


def place():
    group = lax.axis_index("kgrp")
    return lax.div(group, 2), lax.rem(group, 2), lax.axis_index("row"), lax.axis_index("col")


def prep_kernel(levels_ref, rank_ref, times_ref, map_ref, kpoint_ref, weight_ref, pair_ref, slot_of):
    bands = levels_ref.shape[2]
    times = weight_ref.shape[1]
    for kind in range(2):
        for start in range(0, bands, LANES):
            rank = rank_ref[kind, :, start : start + LANES]
            low, high = rank & (LANES - 1), rank // LANES
            picked = jnp.zeros(rank.shape, jnp.float32)
            for piece in range(bands // LANES):
                table = levels_ref[kind, :, piece * LANES : (piece + 1) * LANES]
                found = jnp.take_along_axis(table, low, axis=1)
                picked = jnp.where(high == piece, found, picked)
            for t in range(times):
                value = jnp.exp(-picked * times_ref[t])
                weight_ref[kind, t, :, start : start + LANES] = value
                weight_ref[kind, t, :, bands + start : bands + start + LANES] = value
    transfers, kpoints = map_ref.shape
    per_group = kpoints // lax.axis_size("kgrp")
    group = lax.axis_index("kgrp")

    def relative(slot):
        return (lax.div(slot, per_group) ^ group) * per_group + lax.rem(slot, per_group)

    for slot in range(kpoints):
        slot_of[kpoint_ref[slot]] = slot
    for transfer in range(transfers):
        for slot in range(kpoints):
            source = slot_of[map_ref[transfer, kpoint_ref[slot]]]
            pair_ref[transfer, relative(source)] = relative(jnp.int32(slot))


def flatten_occ_kernel(occ_ref, occ_out):
    for slot in range(occ_out.shape[0]):
        occ_out[slot] = occ_ref[slot].reshape(occ_out.shape[1:])


def flatten_emp_kernel(emp_ref, occ_flat_ref, emp_out, both_out, *part_outs):
    slots = emp_out.shape[0]
    for slot in range(slots):
        panel = emp_ref[slot].reshape(emp_out.shape[1:])
        emp_out[slot] = panel
        part_outs[slot][0] = panel
        both_out[slot] = occ_flat_ref[slot]
        both_out[slots + slot] = panel


def choose():
    x, h, z, _ = place()
    half = lax.axis_size("row") // 2
    near = x == lax.div(z, half)
    inner = (z == half - 1) | (z == half)
    owns = h == lax.rem(z, 2)
    first = h == lax.div(z, half)
    swapped = jnp.where(inner, 1, 2)
    far1 = jnp.where(inner, 3, 5)
    far2 = jnp.where(inner, 4, 6)
    keep = jnp.where(near, jnp.where(owns, 0, swapped), jnp.where(first, far1, far2))
    send = jnp.where(near, jnp.where(owns, swapped, 0), jnp.where(first, far2, far1))
    return keep, send


def part(ref, kind, slots):
    return ref if ref.shape[0] == slots else ref.at[pl.ds(kind * slots, slots)]


def start_copy(source, kind, target, sem):
    slots = target.shape[0]
    if isinstance(source, tuple):
        for slot, piece in enumerate(source):
            pltpu.make_async_copy(piece, target.at[pl.ds(slot, 1)], sem).start()
    else:
        pltpu.make_async_copy(part(source, kind, slots), target, sem).start()


def grouped(refs, cases):
    extra = len(refs) - cases
    if not extra:
        return list(refs)
    return list(refs[:2]) + [tuple(refs[2 : 3 + extra])] + list(refs[3 + extra :])


def pack_kernel(kind, cases, *refs):
    direct, crossed = grouped(refs[: -2 - cases], cases), refs[-2 - cases : -2]
    send_ref, sems = refs[-2:]
    _, send = choose()
    for case in range(cases):

        @pl.when(send == case)
        def _():
            for side, source in enumerate((direct[case], crossed[case])):
                start_copy(source, kind, send_ref.at[side], sems.at[side])

    for side in range(2):
        pltpu.make_async_copy(send_ref.at[side], send_ref.at[side], sems.at[side]).wait()


def pack(kind, direct, crossed, shape):
    return pl.pallas_call(
        functools.partial(pack_kernel, kind, len(crossed)),
        out_shape=jax.ShapeDtypeStruct((2,) + shape, jnp.bfloat16),
        in_specs=[HBM] * (len(direct) + len(crossed)),
        out_specs=VMEM,
        scratch_shapes=[pltpu.SemaphoreType.DMA((2,))],
        compiler_params=LIMIT,
    )(*direct, *crossed)


def load_columns(kind, groups, direct, crossed, recv, last, col_buf, sems):
    keep, _ = choose()

    def fetch(source, k):
        start_copy(source, kind, col_buf.at[k], sems.at[k, 0])

    for k in groups:
        if k & 1:
            inside = recv.at[k >> 1]
            if last is None:
                fetch(inside, k)
            else:
                pl.when(keep == 6)(functools.partial(fetch, last, k))
                pl.when(keep != 6)(functools.partial(fetch, inside, k))
        else:
            for case, source in enumerate((direct, crossed)[k >> 1]):
                pl.when(keep == case)(functools.partial(fetch, source, k))


def load_rows(kind, groups, rows, row_buf, sems):
    slots = row_buf.shape[2]
    for k in groups:
        for half in range(2):
            panel = part(rows[half * 4 + k], kind, slots)
            pltpu.make_async_copy(panel, row_buf.at[half, k], sems.at[k, 1 + half]).start()


def wait_columns(k, col_buf, sems):
    pltpu.make_async_copy(col_buf.at[k], col_buf.at[k], sems.at[k, 0]).wait()


def wait_rows(k, row_buf, sems):
    for half in range(2):
        pltpu.make_async_copy(row_buf.at[half, k], row_buf.at[half, k], sems.at[k, 1 + half]).wait()


def scale_rows(kind, k, i, half, row_buf, weight_ref):
    slot = (lax.axis_index("kgrp") ^ k) * row_buf.shape[2] + i
    panel = row_buf[half, k, i].astype(jnp.float32)
    scaled = [
        (panel * weight_ref[kind, t, pl.ds(slot, 1), :]).astype(jnp.bfloat16)
        for t in range(weight_ref.shape[1])
    ]
    return jnp.concatenate(scaled, axis=0)


def tile(stacked, scaled):
    return lax.dot_general(stacked, scaled, (((1,), (1,)), ((), ())), preferred_element_type=jnp.float32)


def stack_columns(columns):
    width = columns.shape[1] // 2
    turned = jnp.concatenate([-columns[:, width:], columns[:, :width]], axis=1)
    return jnp.concatenate([columns, turned], axis=0)


def occ_kernel(cases, *refs):
    rows, direct, crossed = refs[:8], refs[8 : 8 + cases], refs[8 + cases : 8 + 2 * cases]
    recv, weight_ref, out_ref, row_buf, col_buf, sems = refs[8 + 2 * cases :]
    load_columns(0, range(4), direct, crossed, recv, None, col_buf, sems)
    load_rows(0, range(4), rows, row_buf, sems)
    per_group = col_buf.shape[1]
    for k in range(4):
        wait_columns(k, col_buf, sems)
        wait_rows(k, row_buf, sems)
        for i in range(per_group):
            stacked = stack_columns(col_buf[k, i])
            for half in range(2):
                scaled = scale_rows(0, k, i, half, row_buf, weight_ref)
                out_ref[k * per_group + i, half] = tile(stacked, scaled)


STRIP = 16


def pair_sums(moved, occ_ref, pair_ref, first, before, store):
    count, halves = moved.shape[:2]
    block = moved.shape[2] // 2
    transfers = pair_ref.shape[0]
    held = [[pair_ref[q, first + a] for a in range(count)] for q in range(transfers)]
    for half in range(halves):

        def strip(index, carry):
            real_rows = pl.ds(pl.multiple_of(index * STRIP, STRIP), STRIP)
            imag_rows = pl.ds(pl.multiple_of(index * STRIP + block, STRIP), STRIP)
            sums = [[None, None] for _ in range(transfers)]
            if before is not None:
                sums = [[before[q, half, comp, real_rows, :] for comp in range(2)] for q in range(transfers)]
            for a in range(count):
                re, im = moved[a, half, real_rows, :], moved[a, half, imag_rows, :]
                for q in range(transfers):
                    ro = occ_ref[held[q][a], half, real_rows, :]
                    io = occ_ref[held[q][a], half, imag_rows, :]
                    for comp, piece in enumerate((ro * re + io * im, io * re - ro * im)):
                        sums[q][comp] = piece if sums[q][comp] is None else sums[q][comp] + piece
            for q in range(transfers):
                for comp in range(2):
                    store(half, real_rows, q, comp, sums[q][comp])
            return carry

        lax.fori_loop(0, block // STRIP, strip, 0)


def scale_kernel(*refs):
    rows, weight_ref, scaled_ref, row_buf, sems = refs[:8], *refs[8:]
    load_rows(1, range(4), rows, row_buf, sems)
    for k in range(4):
        wait_rows(k, row_buf, sems)
        for i in range(row_buf.shape[2]):
            for half in range(2):
                scaled_ref[half, k, i] = scale_rows(1, k, i, half, row_buf, weight_ref)


def emp_direct_kernel(cases, *refs):
    direct = grouped(refs[:-8], cases)
    recv, scaled_ref, pair_ref, occ_ref, sum_ref, col_buf, moved, sems = refs[-8:]
    load_columns(1, (0, 1), direct, None, recv, None, col_buf, sems)
    per_group = col_buf.shape[1]
    for k in (0, 1):
        wait_columns(k, col_buf, sems)
        for i in range(per_group):
            stacked = stack_columns(col_buf[k, i])
            for half in range(2):
                moved[k * per_group + i, half] = tile(stacked, scaled_ref[half, k, i])

    def store(half, rows_at, q, comp, value):
        sum_ref[q, half, comp, rows_at, :] = value

    pair_sums(moved, occ_ref, pair_ref, 0, None, store)


def closing_kernel(factor, cases, *refs):
    crossed = refs[:cases]
    recv, last, scaled_ref, pair_ref, occ_ref, sum_ref, out_ref, col_buf, moved, sems = refs[cases:]
    load_columns(1, (2, 3), None, crossed, recv, last, col_buf, sems)
    per_group, block = col_buf.shape[1:3]
    times = out_ref.shape[3]
    y = lax.axis_index("col")
    for k in (2, 3):
        wait_columns(k, col_buf, sems)
        for i in range(per_group):
            stacked = stack_columns(col_buf[k, i])
            for half in range(2):
                moved[(k - 2) * per_group + i, half] = tile(stacked, scaled_ref[half, k, i])

    def store(half, rows_at, q, comp, value):
        start = pl.multiple_of((y ^ half) * block, LANES)
        value = value * factor
        for t in range(times):
            out_ref[comp, q, rows_at, t, pl.ds(start, block)] = value[:, t * block : (t + 1) * block]

    pair_sums(moved, occ_ref, pair_ref, 2 * per_group, sum_ref, store)


def output_stationary(occ_orbitals, emp_orbitals, energies, band_order, imag_times, kq_map, slot_kpoint):
    groups, rows, cols = (lax.axis_size(name) for name in AXES)
    slots, block = occ_orbitals.shape[:2]
    width = occ_orbitals.shape[2] * occ_orbitals.shape[3]
    transfers, times = kq_map.shape[0], imag_times.shape[0]
    kpoints = groups * slots
    half = rows // 2
    top = rows - 1

    def send(array, route):
        pairs = []
        for g in range(groups):
            for z in range(rows):
                for y in range(cols):
                    target = route(g // 2, g % 2, z, y)
                    if target is not None:
                        x2, h2, z2, y2 = target
                        pairs.append(((g * rows + z) * cols + y, ((2 * x2 + h2) * rows + z2) * cols + y2))
        return lax.ppermute(array, AXES, pairs)

    def inner(z):
        return z in (half - 1, half)

    def near(x, z):
        return x == z // half

    def swap(x, h, z, y):
        return x, h, z ^ 1, y

    def swap_main(x, h, z, y):
        return None if inner(z) and near(x, z) else (x, h, z ^ 1, y)

    def swap_late(x, h, z, y):
        return (x, h, z ^ 1, y) if inner(z) and near(x, z) else None

    def middle(x, h, z, y):
        return (x, h, top - z, y) if inner(z) else None

    def outward_near(x, h, z, y):
        return (x, h, z ^ 1, y) if inner(z) and near(x, z) else None

    def outward_far(x, h, z, y):
        return (x, h, z ^ 1, y) if inner(z) and not near(x, z) else None

    def flip_x(x, h, z, y):
        return 1 - x, h, z, y

    def middle_or_to_near(x, h, z, y):
        if inner(z):
            return x, h, top - z, y
        return None if near(x, z) else (1 - x, h, z, y)

    def from_near(x, h, z, y):
        if not near(x, z):
            return None
        return (x, h, top - z, y) if inner(z) else (x, h, z ^ 1, y)

    def to_far_or_outward(x, h, z, y):
        if not inner(z):
            return None
        return (1 - x, h, z, y) if near(x, z) else (x, h, z ^ 1, y)

    def to_far_outer(x, h, z, y):
        return (1 - x, h, z, y) if near(x, z) and not inner(z) else None

    def to_owner(x, h, z, y):
        owner = h != z // half
        return (1 - x, h, z, y) if near(x, z) and not inner(z) and owner else None

    def to_other_owner(x, h, z, y):
        owner = h != z // half
        return None if owner or inner(z) or not near(x, z) else (1 - x, 1 - h, z, y)

    def flip_y(x, h, z, y):
        return x, h, z, 1 - y

    def flip_core(x, h, z, y):
        return x, 1 - h, z, y

    flat = jax.ShapeDtypeStruct((slots, block, width), jnp.bfloat16)
    occ_flat = pl.pallas_call(
        flatten_occ_kernel,
        out_shape=flat,
        in_specs=[VMEM],
        out_specs=VMEM,
        compiler_params=LIMIT,
        name="flatten_occ",
    )(occ_orbitals)
    single = jax.ShapeDtypeStruct((1, block, width), jnp.bfloat16)
    emp_flat, both, *emp_parts = pl.pallas_call(
        flatten_emp_kernel,
        out_shape=[flat, jax.ShapeDtypeStruct((2 * slots, block, width), jnp.bfloat16)] + [single] * slots,
        in_specs=[VMEM] * 2,
        out_specs=[VMEM] * (2 + slots),
        compiler_params=LIMIT,
        name="flatten_emp",
    )(emp_orbitals, occ_flat)
    kinds = [occ_flat, emp_flat]

    prepare = pl.pallas_call(
        prep_kernel,
        out_shape=[
            jax.ShapeDtypeStruct((2, times, kpoints, width), jnp.float32),
            jax.ShapeDtypeStruct((transfers, kpoints), jnp.int32),
        ],
        in_specs=[VMEM, VMEM, SMEM, SMEM, SMEM],
        out_specs=[VMEM, SMEM],
        scratch_shapes=[pltpu.SMEM((kpoints,), jnp.int32)],
        compiler_params=LIMIT,
        name="prep",
    )
    weights, pairs = prepare(energies, band_order, imag_times, kq_map, slot_kpoint)

    s1 = [send(kinds[0], swap), send(kinds[1], swap_main)]
    late = [send(emp_parts[slot], swap_late) for slot in range(slots)]
    b = [send(kinds[i], middle) for i in range(2)]
    crossed = send(both, flip_x)
    turned = send(both, flip_y)
    sibling = send(both, flip_core)
    d = [send(s1[i], middle_or_to_near) for i in range(2)]
    en = [send(b[i], outward_near) for i in range(2)]
    e = [send(b[i], outward_far) for i in range(2)]
    bx = send(crossed, from_near)
    turned_crossed = send(crossed, flip_y)
    crossed_sibling = send(crossed, flip_core)
    turned_sibling = send(turned, flip_core)
    turned_crossed_sibling = send(turned_crossed, flip_core)
    ex = [send(en[i], to_far_outer) for i in range(2)]
    fn = [send(d[i], outward_near) for i in range(2)]
    f = [send(d[i], to_far_or_outward) for i in range(2)]
    fx = [send(fn[0], to_far_outer), send(fn[1], to_owner)]
    last = send(fn[1], to_other_owner)
    row_panels, direct, across, given = [], [], [], []
    for kind in range(2):
        row_panels.append([
            kinds[kind], sibling, crossed, crossed_sibling,
            turned, turned_sibling, turned_crossed, turned_crossed_sibling,
        ])
        swapped = late if kind else s1[:1]
        direct.append([kinds[kind], s1[kind], *swapped, b[kind], d[kind], e[kind], f[kind]])
        across.append([crossed, bx, d[kind], bx, f[kind], ex[kind], fx[kind]])
        ready = across[kind][:-1] + [ex[1] if kind else fx[0]]
        give = pack(kind, direct[kind], ready, (slots, block, width))
        given.append(send(give, flip_core))

    panel_scratch = [
        pltpu.VMEM((2, 4, slots, block, width), jnp.bfloat16),
        pltpu.VMEM((4, slots, block, width), jnp.bfloat16),
    ]
    cases = len(across[0])
    occ_tiles = pl.pallas_call(
        functools.partial(occ_kernel, cases),
        out_shape=jax.ShapeDtypeStruct((kpoints, 2, 2 * block, times * block), jnp.float32),
        in_specs=[HBM] * (9 + 2 * cases) + [VMEM],
        out_specs=VMEM,
        scratch_shapes=panel_scratch + [pltpu.SemaphoreType.DMA((4, 3))],
        compiler_params=LIMIT,
        name="occ_tiles",
    )
    tiles = occ_tiles(*row_panels[0], *direct[0], *across[0], given[0], weights)
    half_tiles = (kpoints // 2, 2, 2 * block, times * block)
    scale = pl.pallas_call(
        scale_kernel,
        out_shape=jax.ShapeDtypeStruct((2, 4, slots, times * block, width), jnp.bfloat16),
        in_specs=[HBM] * 8 + [VMEM],
        out_specs=VMEM,
        scratch_shapes=panel_scratch[:1] + [pltpu.SemaphoreType.DMA((4, 3))],
        compiler_params=LIMIT,
        name="scale",
    )
    scaled = scale(*row_panels[1], weights)
    emp_direct = pl.pallas_call(
        functools.partial(emp_direct_kernel, cases),
        out_shape=jax.ShapeDtypeStruct((transfers, 2, 2, block, times * block), jnp.float32),
        in_specs=[HBM] * (1 + len(direct[1])) + [VMEM, SMEM, VMEM],
        out_specs=VMEM,
        scratch_shapes=panel_scratch[1:] + [pltpu.VMEM(half_tiles, jnp.float32), pltpu.SemaphoreType.DMA((4, 3))],
        compiler_params=LIMIT,
        name="emp_direct",
    )
    sums = emp_direct(*direct[1], given[1], scaled, pairs, tiles)
    result = pl.pallas_call(
        functools.partial(closing_kernel, -1.0 / kpoints, cases),
        out_shape=jax.ShapeDtypeStruct((2, transfers, block, times, cols * block), jnp.float32),
        in_specs=[HBM] * (2 + cases) + [VMEM, SMEM, VMEM, VMEM],
        out_specs=VMEM,
        scratch_shapes=panel_scratch[1:] + [pltpu.VMEM(half_tiles, jnp.float32), pltpu.SemaphoreType.DMA((4, 3))],
        compiler_params=LIMIT,
        name="closing",
    )(*across[1], given[1], last, scaled, pairs, tiles, sums)
    return result[:, :, None]


def staged(*arguments):
    return output_stationary(*arguments)


def solution(mesh):
    in_specs = (
        P("kgrp", ("row", "col"), None, None),
        P("kgrp", ("row", "col"), None, None),
        P(),
        P(),
        P(),
        P(),
        P(),
    )
    out_specs = P(None, None, "col", "kgrp", None, "row")
    groups, rows, cols = (mesh.shape[name] for name in AXES)
    line = groups == rows == 2 * cols == 4
    body = staged if line else summed_over_groups
    return jax.shard_map(body, mesh=mesh, in_specs=in_specs, out_specs=out_specs, check_vma=False)
```

```python
import functools

import jax
import jax.numpy as jnp
from jax import lax
from jax.experimental import pallas as pl
from jax.experimental.pallas import tpu as pltpu
from jax.sharding import PartitionSpec as P


def table_row(lookup_table, wanted):
    positions = jnp.arange(lookup_table.shape[0], dtype=jnp.int32)
    chosen = positions[:, None] == wanted
    return jnp.sum(jnp.where(chosen, lookup_table, jnp.zeros_like(lookup_table)), axis=0)


def band_weights(levels, band_rank, imag_times):
    picked = jnp.take(levels, band_rank, axis=0)
    return jnp.exp(-picked[None, :] * imag_times[:, None])


def green_tile(row_panel, col_panel, weights):
    times_count = weights.shape[0]
    scaled = (row_panel[None] * weights[:, None, None, :]).astype(jnp.bfloat16)
    scaled = scaled.reshape(times_count, row_panel.shape[0], -1)
    turned = jnp.concatenate([-col_panel[:, 1], col_panel[:, 0]], axis=1)
    stacked = jnp.concatenate([col_panel.reshape(col_panel.shape[0], -1), turned], axis=0)
    result = lax.dot_general(
        stacked, scaled, (((1,), (2,)), ((), ())), preferred_element_type=jnp.float32
    )
    return result.reshape(2, col_panel.shape[0], times_count, row_panel.shape[0])


def pair_term(held_tile, moved_tile, factor):
    real_part = held_tile[0] * moved_tile[0] + held_tile[1] * moved_tile[1]
    imag_part = held_tile[1] * moved_tile[0] - held_tile[0] * moved_tile[1]
    return factor * jnp.stack([real_part, imag_part])


def source_slots(kq_map, slot_kpoint, own_slots):
    positions = jnp.arange(slot_kpoint.shape[0], dtype=jnp.int32)
    own_kpoint = jnp.sum(
        jnp.where(own_slots[:, None] == positions[None, :], slot_kpoint[None, :], 0), axis=1
    )
    target = jnp.sum(
        jnp.where(own_kpoint[None, :, None] == positions[None, None, :], kq_map[:, None, :], 0),
        axis=2,
    )
    return jnp.sum(
        jnp.where(target[:, :, None] == slot_kpoint[None, None, :], positions[None, None, :], 0),
        axis=2,
    )


def summed_over_groups(occ_orbitals, emp_orbitals, energies, band_order, imag_times, kq_map, slot_kpoint):
    groups = lax.axis_size("kgrp")
    per_group = occ_orbitals.shape[0]
    kpoints = groups * per_group
    transfers = kq_map.shape[0]
    factor = -1.0 / kpoints
    own_slots = lax.axis_index("kgrp") * per_group + jnp.arange(per_group, dtype=jnp.int32)
    sources = source_slots(kq_map, slot_kpoint, own_slots)
    flat_sources = sources.reshape(-1)
    initial = jnp.zeros((flat_sources.shape[0],) + emp_orbitals.shape[1:], jnp.float32)
    block_part = lax.all_gather(emp_orbitals, "kgrp", axis=0, tiled=True)
    numbered = block_part.shape[0]
    matches = (flat_sources[:, None] == jnp.arange(numbered, dtype=jnp.int32)[None, :]).astype(
        jnp.bfloat16
    )
    update = jnp.dot(matches, block_part.reshape(numbered, -1), preferred_element_type=jnp.float32)
    fetched = update.reshape(initial.shape).astype(jnp.bfloat16)
    occ_rows, emp_rows = (
        lax.all_gather(occ_orbitals, "col", axis=1, tiled=True),
        lax.all_gather(fetched, "col", axis=1, tiled=True),
    )
    occ_cols, emp_cols = (
        lax.all_gather(occ_orbitals, "row", axis=1, tiled=True),
        lax.all_gather(fetched, "row", axis=1, tiled=True),
    )
    tiles = []
    for position in range(per_group):
        weights = band_weights(
            table_row(energies[0], own_slots[position]),
            table_row(band_order[0], own_slots[position]),
            imag_times,
        )
        tiles.append(green_tile(occ_rows[position], occ_cols[position], weights))

    def transfer_terms(transfer):
        partial_value = None
        for position in range(per_group):
            source = sources[transfer, position]
            weights = band_weights(
                table_row(energies[1], source), table_row(band_order[1], source), imag_times
            )
            moved_index = transfer * per_group + position
            moved_tile = green_tile(emp_rows[moved_index], emp_cols[moved_index], weights)
            addition = pair_term(tiles[position], moved_tile, factor)
            partial_value = addition if partial_value is None else partial_value + addition
        return partial_value

    terms_all = jnp.stack([transfer_terms(transfer) for transfer in range(transfers)], axis=1)
    summed = lax.psum_scatter(terms_all, "kgrp", scatter_dimension=2, tiled=True)
    return summed[:, :, None]


LANES = 128
HBM = pl.BlockSpec(memory_space=pltpu.HBM)
VMEM = pl.BlockSpec(memory_space=pltpu.VMEM)
SMEM = pl.BlockSpec(memory_space=pltpu.SMEM)
LIMIT = pltpu.CompilerParams(vmem_limit_bytes=16 * 2**20)
AXES = ("kgrp", "row", "col")


def place():
    group = lax.axis_index("kgrp")
    return lax.div(group, 2), lax.rem(group, 2), lax.axis_index("row"), lax.axis_index("col")


def prep_kernel(levels_in, rank_in, times_ref, map_ref, kpoint_ref, weight_ref, pair_ref, slot_of, levels_ref, rank_ref, sems):
    copies = [
        pltpu.make_async_copy(levels_in, levels_ref, sems.at[0]),
        pltpu.make_async_copy(rank_in, rank_ref, sems.at[1]),
    ]
    for copy in copies:
        copy.start()
    for copy in copies:
        copy.wait()
    bands = levels_ref.shape[2]
    times = weight_ref.shape[1]
    for kind in range(2):
        for start in range(0, bands, LANES):
            rank = rank_ref[kind, :, start : start + LANES]
            low, high = rank & (LANES - 1), rank // LANES
            picked = jnp.zeros(rank.shape, jnp.float32)
            for piece in range(bands // LANES):
                table = levels_ref[kind, :, piece * LANES : (piece + 1) * LANES]
                found = jnp.take_along_axis(table, low, axis=1)
                picked = jnp.where(high == piece, found, picked)
            for t in range(times):
                value = jnp.exp(-picked * times_ref[t])
                weight_ref[kind, t, :, start : start + LANES] = value
                weight_ref[kind, t, :, bands + start : bands + start + LANES] = value
    transfers, kpoints = map_ref.shape
    per_group = kpoints // lax.axis_size("kgrp")
    group = lax.axis_index("kgrp")

    def relative(slot):
        return (lax.div(slot, per_group) ^ group) * per_group + lax.rem(slot, per_group)

    for slot in range(kpoints):
        slot_of[kpoint_ref[slot]] = slot
    for transfer in range(transfers):
        for slot in range(kpoints):
            source = slot_of[map_ref[transfer, kpoint_ref[slot]]]
            pair_ref[transfer, relative(source)] = relative(jnp.int32(slot))


def flatten_occ_kernel(occ_ref, occ_out):
    for slot in range(occ_out.shape[0]):
        occ_out[slot] = occ_ref[slot].reshape(occ_out.shape[1:])


def flatten_emp_kernel(emp_ref, occ_flat_ref, emp_out, both_out, *part_outs):
    slots = emp_out.shape[0]
    for slot in range(slots):
        panel = emp_ref[slot].reshape(emp_out.shape[1:])
        emp_out[slot] = panel
        part_outs[slot][0] = panel
        both_out[slot] = occ_flat_ref[slot]
        both_out[slots + slot] = panel


def choose():
    x, h, z, _ = place()
    half = lax.axis_size("row") // 2
    near = x == lax.div(z, half)
    inner = (z == half - 1) | (z == half)
    owns = h == lax.rem(z, 2)
    first = h == lax.div(z, half)
    swapped = jnp.where(inner, 1, 2)
    far1 = jnp.where(inner, 3, 5)
    far2 = jnp.where(inner, 4, 6)
    keep = jnp.where(near, jnp.where(owns, 0, swapped), jnp.where(first, far1, far2))
    send = jnp.where(near, jnp.where(owns, swapped, 0), jnp.where(first, far2, far1))
    return keep, send


def part(ref, kind, slots):
    return ref if ref.shape[0] == slots else ref.at[pl.ds(kind * slots, slots)]


def start_copy(source, kind, target, sem):
    slots = target.shape[0]
    if isinstance(source, tuple):
        for slot, piece in enumerate(source):
            pltpu.make_async_copy(piece, target.at[pl.ds(slot, 1)], sem).start()
    else:
        pltpu.make_async_copy(part(source, kind, slots), target, sem).start()


def grouped(refs, cases):
    extra = len(refs) - cases
    if not extra:
        return list(refs)
    return list(refs[:2]) + [tuple(refs[2 : 3 + extra])] + list(refs[3 + extra :])


def pack_kernel(kind, cases, *refs):
    direct, crossed = grouped(refs[: -2 - cases], cases), refs[-2 - cases : -2]
    send_ref, sems = refs[-2:]
    _, send = choose()
    for case in range(cases):

        @pl.when(send == case)
        def _():
            for side, source in enumerate((direct[case], crossed[case])):
                start_copy(source, kind, send_ref.at[side], sems.at[side])

    for side in range(2):
        pltpu.make_async_copy(send_ref.at[side], send_ref.at[side], sems.at[side]).wait()


def pack(kind, direct, crossed, shape):
    return pl.pallas_call(
        functools.partial(pack_kernel, kind, len(crossed)),
        out_shape=jax.ShapeDtypeStruct((2,) + shape, jnp.bfloat16),
        in_specs=[HBM] * (len(direct) + len(crossed)),
        out_specs=VMEM,
        scratch_shapes=[pltpu.SemaphoreType.DMA((2,))],
        compiler_params=LIMIT,
    )(*direct, *crossed)


def load_columns(kind, groups, direct, crossed, recv, last, col_buf, sems):
    keep, _ = choose()

    def fetch(source, k):
        start_copy(source, kind, col_buf.at[k], sems.at[k, 0])

    for k in groups:
        if k & 1:
            inside = recv.at[k >> 1]
            if last is None or k == 1:
                fetch(inside, k)
            else:
                pl.when(keep == 6)(functools.partial(fetch, last, k))
                pl.when(keep != 6)(functools.partial(fetch, inside, k))
        else:
            for case, source in enumerate((direct, crossed)[k >> 1]):
                pl.when(keep == case)(functools.partial(fetch, source, k))


def load_rows(kind, groups, rows, row_buf, sems):
    slots = row_buf.shape[2]
    for k in groups:
        for half in range(2):
            panel = part(rows[half * 4 + k], kind, slots)
            pltpu.make_async_copy(panel, row_buf.at[half, k], sems.at[k, 1 + half]).start()


def wait_columns(k, col_buf, sems):
    pltpu.make_async_copy(col_buf.at[k], col_buf.at[k], sems.at[k, 0]).wait()


def wait_rows(k, row_buf, sems):
    for half in range(2):
        pltpu.make_async_copy(row_buf.at[half, k], row_buf.at[half, k], sems.at[k, 1 + half]).wait()


def scale_rows(kind, k, i, half, row_buf, weight_ref):
    slot = (lax.axis_index("kgrp") ^ k) * row_buf.shape[2] + i
    panel = row_buf[half, k, i].astype(jnp.float32)
    scaled = [
        (panel * weight_ref[kind, t, pl.ds(slot, 1), :]).astype(jnp.bfloat16)
        for t in range(weight_ref.shape[1])
    ]
    return jnp.concatenate(scaled, axis=0)


def tile(stacked, scaled):
    return lax.dot_general(stacked, scaled, (((1,), (1,)), ((), ())), preferred_element_type=jnp.float32)


def stack_columns(columns):
    width = columns.shape[1] // 2
    turned = jnp.concatenate([-columns[:, width:], columns[:, :width]], axis=1)
    return jnp.concatenate([columns, turned], axis=0)


def occ_kernel(cases, *refs):
    direct, crossed = refs[:cases], refs[cases : 2 * cases]
    recv, last, scaled_ref, out_ref, col_buf, sems = refs[2 * cases :]
    load_columns(0, range(4), direct, crossed, recv, last, col_buf, sems)
    per_group = col_buf.shape[1]
    for k in range(4):
        wait_columns(k, col_buf, sems)
        for i in range(per_group):
            stacked = stack_columns(col_buf[k, i])
            for half in range(2):
                out_ref[k * per_group + i, half] = tile(stacked, scaled_ref[half, k, i])


STRIP = 16


def pair_sums(moved, occ_ref, pair_ref, first, before, store):
    count, halves = moved.shape[:2]
    block = moved.shape[2] // 2
    transfers = pair_ref.shape[0]
    held = [[pair_ref[q, first + a] for a in range(count)] for q in range(transfers)]
    for half in range(halves):

        def strip(index, carry):
            real_rows = pl.ds(pl.multiple_of(index * STRIP, STRIP), STRIP)
            imag_rows = pl.ds(pl.multiple_of(index * STRIP + block, STRIP), STRIP)
            sums = [[None, None] for _ in range(transfers)]
            if before is not None:
                sums = [[before[q, half, comp, real_rows, :] for comp in range(2)] for q in range(transfers)]
            for a in range(count):
                re, im = moved[a, half, real_rows, :], moved[a, half, imag_rows, :]
                for q in range(transfers):
                    ro = occ_ref[held[q][a], half, real_rows, :]
                    io = occ_ref[held[q][a], half, imag_rows, :]
                    for comp, piece in enumerate((ro * re + io * im, io * re - ro * im)):
                        sums[q][comp] = piece if sums[q][comp] is None else sums[q][comp] + piece
            for q in range(transfers):
                for comp in range(2):
                    store(half, real_rows, q, comp, sums[q][comp])
            return carry

        lax.fori_loop(0, block // STRIP, strip, 0)


def scale_kernel(kind, *refs):
    rows, weight_ref, scaled_ref, row_buf, sems = refs[:8], *refs[8:]
    load_rows(kind, range(4), rows, row_buf, sems)
    for k in range(4):
        wait_rows(k, row_buf, sems)
        for i in range(row_buf.shape[2]):
            for half in range(2):
                scaled_ref[half, k, i] = scale_rows(kind, k, i, half, row_buf, weight_ref)


def emp_direct_kernel(cases, *refs):
    direct = grouped(refs[:-8], cases)
    recv, scaled_ref, pair_ref, occ_ref, sum_ref, col_buf, moved, sems = refs[-8:]
    load_columns(1, (0, 1), direct, None, recv, None, col_buf, sems)
    per_group = col_buf.shape[1]
    for k in (0, 1):
        wait_columns(k, col_buf, sems)
        for i in range(per_group):
            stacked = stack_columns(col_buf[k, i])
            for half in range(2):
                moved[k * per_group + i, half] = tile(stacked, scaled_ref[half, k, i])

    def store(half, rows_at, q, comp, value):
        sum_ref[q, half, comp, rows_at, :] = value

    pair_sums(moved, occ_ref, pair_ref, 0, None, store)


def closing_kernel(factor, cases, *refs):
    crossed = list(refs[: cases - 1]) + [refs[cases - 1 : cases + 1]]
    recv, scaled_ref, pair_ref, occ_ref, sum_ref, out_ref, col_buf, moved, sems = refs[cases + 1 : cases + 2] + refs[cases + 4 :]
    last = refs[cases + 2 : cases + 4]
    load_columns(1, (2, 3), None, crossed, recv, last, col_buf, sems)
    per_group, block = col_buf.shape[1:3]
    times = out_ref.shape[3]
    y = lax.axis_index("col")
    for k in (2, 3):
        wait_columns(k, col_buf, sems)
        for i in range(per_group):
            stacked = stack_columns(col_buf[k, i])
            for half in range(2):
                moved[(k - 2) * per_group + i, half] = tile(stacked, scaled_ref[half, k, i])

    def store(half, rows_at, q, comp, value):
        start = pl.multiple_of((y ^ half) * block, LANES)
        value = value * factor
        for t in range(times):
            out_ref[comp, q, rows_at, t, pl.ds(start, block)] = value[:, t * block : (t + 1) * block]

    pair_sums(moved, occ_ref, pair_ref, 2 * per_group, sum_ref, store)


def output_stationary(occ_orbitals, emp_orbitals, energies, band_order, imag_times, kq_map, slot_kpoint):
    groups, rows, cols = (lax.axis_size(name) for name in AXES)
    slots, block = occ_orbitals.shape[:2]
    width = occ_orbitals.shape[2] * occ_orbitals.shape[3]
    transfers, times = kq_map.shape[0], imag_times.shape[0]
    kpoints = groups * slots
    half = rows // 2
    top = rows - 1

    def send(array, route):
        pairs = []
        for g in range(groups):
            for z in range(rows):
                for y in range(cols):
                    target = route(g // 2, g % 2, z, y)
                    if target is not None:
                        x2, h2, z2, y2 = target
                        pairs.append(((g * rows + z) * cols + y, ((2 * x2 + h2) * rows + z2) * cols + y2))
        return lax.ppermute(array, AXES, pairs)

    def inner(z):
        return z in (half - 1, half)

    def near(x, z):
        return x == z // half

    def swap(x, h, z, y):
        return x, h, z ^ 1, y

    def swap_main(x, h, z, y):
        return None if inner(z) and near(x, z) else (x, h, z ^ 1, y)

    def swap_late(x, h, z, y):
        return (x, h, z ^ 1, y) if inner(z) and near(x, z) else None

    def middle(x, h, z, y):
        return (x, h, top - z, y) if inner(z) else None

    def outward_near(x, h, z, y):
        return (x, h, z ^ 1, y) if inner(z) and near(x, z) else None

    def outward_far(x, h, z, y):
        return (x, h, z ^ 1, y) if inner(z) and not near(x, z) else None

    def flip_x(x, h, z, y):
        return 1 - x, h, z, y

    def middle_or_to_near(x, h, z, y):
        if inner(z):
            return x, h, top - z, y
        return None if near(x, z) else (1 - x, h, z, y)

    def from_near(x, h, z, y):
        if not near(x, z):
            return None
        return (x, h, top - z, y) if inner(z) else (x, h, z ^ 1, y)

    def inward_near(x, h, z, y):
        return (x, h, z ^ 1, y) if near(x, z) and not inner(z) else None

    def to_far_or_outward(x, h, z, y):
        if not inner(z):
            return None
        return (1 - x, h, z, y) if near(x, z) else (x, h, z ^ 1, y)

    def to_far_outer(x, h, z, y):
        return (1 - x, h, z, y) if near(x, z) and not inner(z) else None

    def to_owner(x, h, z, y):
        owner = h != z // half
        return (1 - x, h, z, y) if near(x, z) and not inner(z) and owner else None

    def to_other_owner(x, h, z, y):
        owner = h != z // half
        return None if owner or inner(z) or not near(x, z) else (1 - x, 1 - h, z, y)

    def outward_owner(x, h, z, y):
        owner = h != z // half
        return (x, h, z ^ 1, y) if inner(z) and not near(x, z) and owner else None

    def outward_other(x, h, z, y):
        owner = h != z // half
        return None if owner or near(x, z) or not inner(z) else (x, 1 - h, z ^ 1, y)

    def to_far_inner(x, h, z, y):
        return (1 - x, h, z, y) if near(x, z) and inner(z) else None

    def flip_y(x, h, z, y):
        return x, h, z, 1 - y

    def flip_core(x, h, z, y):
        return x, 1 - h, z, y

    flat = jax.ShapeDtypeStruct((slots, block, width), jnp.bfloat16)
    occ_flat = pl.pallas_call(
        flatten_occ_kernel,
        out_shape=flat,
        in_specs=[VMEM],
        out_specs=VMEM,
        compiler_params=LIMIT,
        name="flatten_occ",
    )(occ_orbitals)
    single = jax.ShapeDtypeStruct((1, block, width), jnp.bfloat16)
    emp_flat, both, *emp_parts = pl.pallas_call(
        flatten_emp_kernel,
        out_shape=[flat, jax.ShapeDtypeStruct((2 * slots, block, width), jnp.bfloat16)] + [single] * slots,
        in_specs=[VMEM] * 2,
        out_specs=[VMEM] * (2 + slots),
        compiler_params=LIMIT,
        name="flatten_emp",
    )(emp_orbitals, occ_flat)
    kinds = [occ_flat, emp_flat]

    prepare = pl.pallas_call(
        prep_kernel,
        out_shape=[
            jax.ShapeDtypeStruct((2, times, kpoints, width), jnp.float32),
            jax.ShapeDtypeStruct((transfers, kpoints), jnp.int32),
        ],
        in_specs=[HBM, HBM, SMEM, SMEM, SMEM],
        out_specs=[VMEM, SMEM],
        scratch_shapes=[
            pltpu.SMEM((kpoints,), jnp.int32),
            pltpu.VMEM(energies.shape, energies.dtype),
            pltpu.VMEM(band_order.shape, band_order.dtype),
            pltpu.SemaphoreType.DMA((2,)),
        ],
        compiler_params=LIMIT,
        name="prep",
    )
    weights, pairs = prepare(energies, band_order, imag_times, kq_map, slot_kpoint)

    s1 = [send(kinds[0], swap), send(kinds[1], swap_main)]
    late = [send(emp_parts[slot], swap_late) for slot in range(slots)]
    b = [send(kinds[i], middle) for i in range(2)]
    crossed = send(both, flip_x)
    turned = send(both, flip_y)
    sibling = send(both, flip_core)
    d = [send(s1[i], middle_or_to_near) for i in range(2)]
    en = [send(b[i], outward_near) for i in range(2)]
    e = [send(b[0], to_far_or_outward), send(b[1], outward_far)]
    bx = [send(crossed[:slots], inward_near), send(crossed[slots:], from_near)]
    turned_crossed = send(crossed, flip_y)
    crossed_sibling = send(crossed, flip_core)
    turned_sibling = send(turned, flip_core)
    turned_crossed_sibling = send(turned_crossed, flip_core)
    ex = [send(en[i], to_far_outer) for i in range(2)]
    head = slots // 2
    fn = [send(d[0], outward_near), send(d[1][:head], outward_near)]
    f = [send(d[0], to_far_or_outward), send(d[1], outward_far)]
    dx = [f[0], send(d[1], to_far_inner)]
    fx = [send(fn[0], to_owner), send(fn[1], to_owner)]
    rest = dx[1][head:]
    last = [[send(fn[0], to_other_owner)], [send(fn[1], to_other_owner), send(rest, outward_other)]]
    outer_rest = send(rest, outward_owner)
    row_panels, direct, across, given = [], [], [], []
    for kind in range(2):
        row_panels.append([
            kinds[kind], sibling, crossed, crossed_sibling,
            turned, turned_sibling, turned_crossed, turned_crossed_sibling,
        ])
        swapped = late if kind else s1[:1]
        direct.append([kinds[kind], s1[kind], *swapped, b[kind], d[kind], e[kind], f[kind]])
        across.append([crossed, bx[kind], d[kind], bx[1] if kind else e[0], dx[kind], ex[kind], fx[kind]] + [outer_rest] * kind)
        ready = across[kind][:6] + [ex[kind]]
        give = pack(kind, direct[kind], ready, (slots, block, width))
        given.append(send(give, flip_core))

    panel_scratch = [
        pltpu.VMEM((2, 4, slots, block, width), jnp.bfloat16),
        pltpu.VMEM((4, slots, block, width), jnp.bfloat16),
    ]
    cases = len(across[0])
    scaled = []
    for kind in range(2):
        scale = pl.pallas_call(
            functools.partial(scale_kernel, kind),
            out_shape=jax.ShapeDtypeStruct((2, 4, slots, times * block, width), jnp.bfloat16),
            in_specs=[HBM] * 8 + [VMEM],
            out_specs=VMEM,
            scratch_shapes=panel_scratch[:1] + [pltpu.SemaphoreType.DMA((4, 3))],
            compiler_params=LIMIT,
        )
        scaled.append(scale(*row_panels[kind], weights))
    occ_tiles = pl.pallas_call(
        functools.partial(occ_kernel, cases),
        out_shape=jax.ShapeDtypeStruct((kpoints, 2, 2 * block, times * block), jnp.float32),
        in_specs=[HBM] * (2 + 2 * cases) + [VMEM],
        out_specs=VMEM,
        scratch_shapes=panel_scratch[1:] + [pltpu.SemaphoreType.DMA((4, 3))],
        compiler_params=LIMIT,
        name="occ_tiles",
    )
    tiles = occ_tiles(*direct[0], *across[0], given[0], *last[0], scaled[0])
    half_tiles = (kpoints // 2, 2, 2 * block, times * block)
    emp_direct = pl.pallas_call(
        functools.partial(emp_direct_kernel, cases),
        out_shape=jax.ShapeDtypeStruct((transfers, 2, 2, block, times * block), jnp.float32),
        in_specs=[HBM] * (1 + len(direct[1])) + [VMEM, SMEM, VMEM],
        out_specs=VMEM,
        scratch_shapes=panel_scratch[1:] + [pltpu.VMEM(half_tiles, jnp.float32), pltpu.SemaphoreType.DMA((4, 3))],
        compiler_params=LIMIT,
        name="emp_direct",
    )
    sums = emp_direct(*direct[1], given[1], scaled[1], pairs, tiles)
    result = pl.pallas_call(
        functools.partial(closing_kernel, -1.0 / kpoints, cases),
        out_shape=jax.ShapeDtypeStruct((2, transfers, block, times, cols * block), jnp.float32),
        in_specs=[HBM] * (4 + cases) + [VMEM, SMEM, VMEM, VMEM],
        out_specs=VMEM,
        scratch_shapes=panel_scratch[1:] + [pltpu.VMEM(half_tiles, jnp.float32), pltpu.SemaphoreType.DMA((4, 3))],
        compiler_params=LIMIT,
        name="closing",
    )(*across[1], given[1], *last[1], scaled[1], pairs, tiles, sums)
    return result[:, :, None]


def staged(*arguments):
    return output_stationary(*arguments)


def solution(mesh):
    in_specs = (
        P("kgrp", ("row", "col"), None, None),
        P("kgrp", ("row", "col"), None, None),
        P(),
        P(),
        P(),
        P(),
        P(),
    )
    out_specs = P(None, None, "col", "kgrp", None, "row")
    groups, rows, cols = (mesh.shape[name] for name in AXES)
    line = groups == rows == 2 * cols == 4
    body = staged if line else summed_over_groups
    return jax.shard_map(body, mesh=mesh, in_specs=in_specs, out_specs=out_specs, check_vma=False)
```

```python
import functools

import jax
import jax.numpy as jnp
from jax import lax
from jax.experimental import pallas as pl
from jax.experimental.pallas import tpu as pltpu
from jax.sharding import PartitionSpec as P


def table_row(lookup_table, wanted):
    positions = jnp.arange(lookup_table.shape[0], dtype=jnp.int32)
    chosen = positions[:, None] == wanted
    return jnp.sum(jnp.where(chosen, lookup_table, jnp.zeros_like(lookup_table)), axis=0)


def band_weights(levels, band_rank, imag_times):
    picked = jnp.take(levels, band_rank, axis=0)
    return jnp.exp(-picked[None, :] * imag_times[:, None])


def green_tile(row_panel, col_panel, weights):
    times_count = weights.shape[0]
    scaled = (row_panel[None] * weights[:, None, None, :]).astype(jnp.bfloat16)
    scaled = scaled.reshape(times_count, row_panel.shape[0], -1)
    turned = jnp.concatenate([-col_panel[:, 1], col_panel[:, 0]], axis=1)
    stacked = jnp.concatenate([col_panel.reshape(col_panel.shape[0], -1), turned], axis=0)
    result = lax.dot_general(
        stacked, scaled, (((1,), (2,)), ((), ())), preferred_element_type=jnp.float32
    )
    return result.reshape(2, col_panel.shape[0], times_count, row_panel.shape[0])


def pair_term(held_tile, moved_tile, factor):
    real_part = held_tile[0] * moved_tile[0] + held_tile[1] * moved_tile[1]
    imag_part = held_tile[1] * moved_tile[0] - held_tile[0] * moved_tile[1]
    return factor * jnp.stack([real_part, imag_part])


def source_slots(kq_map, slot_kpoint, own_slots):
    positions = jnp.arange(slot_kpoint.shape[0], dtype=jnp.int32)
    own_kpoint = jnp.sum(
        jnp.where(own_slots[:, None] == positions[None, :], slot_kpoint[None, :], 0), axis=1
    )
    target = jnp.sum(
        jnp.where(own_kpoint[None, :, None] == positions[None, None, :], kq_map[:, None, :], 0),
        axis=2,
    )
    return jnp.sum(
        jnp.where(target[:, :, None] == slot_kpoint[None, None, :], positions[None, None, :], 0),
        axis=2,
    )


def summed_over_groups(occ_orbitals, emp_orbitals, energies, band_order, imag_times, kq_map, slot_kpoint):
    groups = lax.axis_size("kgrp")
    per_group = occ_orbitals.shape[0]
    kpoints = groups * per_group
    transfers = kq_map.shape[0]
    factor = -1.0 / kpoints
    own_slots = lax.axis_index("kgrp") * per_group + jnp.arange(per_group, dtype=jnp.int32)
    sources = source_slots(kq_map, slot_kpoint, own_slots)
    flat_sources = sources.reshape(-1)
    initial = jnp.zeros((flat_sources.shape[0],) + emp_orbitals.shape[1:], jnp.float32)
    block_part = lax.all_gather(emp_orbitals, "kgrp", axis=0, tiled=True)
    numbered = block_part.shape[0]
    matches = (flat_sources[:, None] == jnp.arange(numbered, dtype=jnp.int32)[None, :]).astype(
        jnp.bfloat16
    )
    update = jnp.dot(matches, block_part.reshape(numbered, -1), preferred_element_type=jnp.float32)
    fetched = update.reshape(initial.shape).astype(jnp.bfloat16)
    occ_rows, emp_rows = (
        lax.all_gather(occ_orbitals, "col", axis=1, tiled=True),
        lax.all_gather(fetched, "col", axis=1, tiled=True),
    )
    occ_cols, emp_cols = (
        lax.all_gather(occ_orbitals, "row", axis=1, tiled=True),
        lax.all_gather(fetched, "row", axis=1, tiled=True),
    )
    tiles = []
    for position in range(per_group):
        weights = band_weights(
            table_row(energies[0], own_slots[position]),
            table_row(band_order[0], own_slots[position]),
            imag_times,
        )
        tiles.append(green_tile(occ_rows[position], occ_cols[position], weights))

    def transfer_terms(transfer):
        partial_value = None
        for position in range(per_group):
            source = sources[transfer, position]
            weights = band_weights(
                table_row(energies[1], source), table_row(band_order[1], source), imag_times
            )
            moved_index = transfer * per_group + position
            moved_tile = green_tile(emp_rows[moved_index], emp_cols[moved_index], weights)
            addition = pair_term(tiles[position], moved_tile, factor)
            partial_value = addition if partial_value is None else partial_value + addition
        return partial_value

    terms_all = jnp.stack([transfer_terms(transfer) for transfer in range(transfers)], axis=1)
    summed = lax.psum_scatter(terms_all, "kgrp", scatter_dimension=2, tiled=True)
    return summed[:, :, None]


LANES = 128
HBM = pl.BlockSpec(memory_space=pltpu.HBM)
VMEM = pl.BlockSpec(memory_space=pltpu.VMEM)
SMEM = pl.BlockSpec(memory_space=pltpu.SMEM)
LIMIT = pltpu.CompilerParams(vmem_limit_bytes=16 * 2**20)
AXES = ("kgrp", "row", "col")


def place():
    group = lax.axis_index("kgrp")
    return lax.div(group, 2), lax.rem(group, 2), lax.axis_index("row"), lax.axis_index("col")


def prep_kernel(levels_in, rank_in, times_ref, map_ref, kpoint_ref, weight_ref, pair_ref, slot_of, levels_ref, rank_ref, sems):
    copies = [
        pltpu.make_async_copy(levels_in, levels_ref, sems.at[0]),
        pltpu.make_async_copy(rank_in, rank_ref, sems.at[1]),
    ]
    for copy in copies:
        copy.start()
    for copy in copies:
        copy.wait()
    bands = levels_ref.shape[2]
    times = weight_ref.shape[1]
    for kind in range(2):
        for start in range(0, bands, LANES):
            rank = rank_ref[kind, :, start : start + LANES]
            low, high = rank & (LANES - 1), rank // LANES
            picked = jnp.zeros(rank.shape, jnp.float32)
            for piece in range(bands // LANES):
                table = levels_ref[kind, :, piece * LANES : (piece + 1) * LANES]
                found = jnp.take_along_axis(table, low, axis=1)
                picked = jnp.where(high == piece, found, picked)
            for t in range(times):
                value = jnp.exp(-picked * times_ref[t])
                weight_ref[kind, t, :, start : start + LANES] = value
                weight_ref[kind, t, :, bands + start : bands + start + LANES] = value
    transfers, kpoints = map_ref.shape
    per_group = kpoints // lax.axis_size("kgrp")
    group = lax.axis_index("kgrp")

    def relative(slot):
        return (lax.div(slot, per_group) ^ group) * per_group + lax.rem(slot, per_group)

    for slot in range(kpoints):
        slot_of[kpoint_ref[slot]] = slot
    for transfer in range(transfers):
        for slot in range(kpoints):
            source = slot_of[map_ref[transfer, kpoint_ref[slot]]]
            pair_ref[transfer, relative(source)] = relative(jnp.int32(slot))


def flatten_occ_kernel(occ_ref, occ_out):
    for slot in range(occ_out.shape[0]):
        occ_out[slot] = occ_ref[slot].reshape(occ_out.shape[1:])


def flatten_emp_kernel(emp_ref, occ_flat_ref, emp_out, both_out, *part_outs):
    slots = emp_out.shape[0]
    for slot in range(slots):
        panel = emp_ref[slot].reshape(emp_out.shape[1:])
        emp_out[slot] = panel
        part_outs[slot][0] = panel
        both_out[slot] = occ_flat_ref[slot]
        both_out[slots + slot] = panel


def choose():
    x, h, z, _ = place()
    half = lax.axis_size("row") // 2
    near = x == lax.div(z, half)
    inner = (z == half - 1) | (z == half)
    owns = h == lax.rem(z, 2)
    first = h == lax.div(z, half)
    swapped = jnp.where(inner, 1, 2)
    far1 = jnp.where(inner, 3, 5)
    far2 = jnp.where(inner, 4, 6)
    keep = jnp.where(near, jnp.where(owns, 0, swapped), jnp.where(first, far1, far2))
    send = jnp.where(near, jnp.where(owns, swapped, 0), jnp.where(first, far2, far1))
    return keep, send


def part(ref, kind, slots):
    return ref if ref.shape[0] == slots else ref.at[pl.ds(kind * slots, slots)]


def start_copy(source, kind, target, sem):
    slots = target.shape[0]
    if isinstance(source, tuple):
        for slot, piece in enumerate(source):
            pltpu.make_async_copy(piece, target.at[pl.ds(slot, 1)], sem).start()
    else:
        pltpu.make_async_copy(part(source, kind, slots), target, sem).start()


def grouped(refs, cases):
    extra = len(refs) - cases
    if not extra:
        return list(refs)
    return list(refs[:2]) + [tuple(refs[2 : 3 + extra])] + list(refs[3 + extra :])


def pack_kernel(kind, cases, *refs):
    direct, crossed = grouped(refs[: -2 - cases], cases), refs[-2 - cases : -2]
    send_ref, sems = refs[-2:]
    _, send = choose()
    for case in range(cases):

        @pl.when(send == case)
        def _():
            for side, source in enumerate((direct[case], crossed[case])):
                start_copy(source, kind, send_ref.at[side], sems.at[side])

    for side in range(2):
        pltpu.make_async_copy(send_ref.at[side], send_ref.at[side], sems.at[side]).wait()


def pack(kind, direct, crossed, shape):
    return pl.pallas_call(
        functools.partial(pack_kernel, kind, len(crossed)),
        out_shape=jax.ShapeDtypeStruct((2,) + shape, jnp.bfloat16),
        in_specs=[HBM] * (len(direct) + len(crossed)),
        out_specs=VMEM,
        scratch_shapes=[pltpu.SemaphoreType.DMA((2,))],
        compiler_params=LIMIT,
    )(*direct, *crossed)


def load_columns(kind, groups, direct, crossed, recv, last, col_buf, sems):
    keep, _ = choose()

    def fetch(source, k):
        start_copy(source, kind, col_buf.at[k], sems.at[k, 0])

    for k in groups:
        if k & 1:
            inside = recv.at[k >> 1]
            if last is None or k == 1:
                fetch(inside, k)
            else:
                pl.when(keep == 6)(functools.partial(fetch, last, k))
                pl.when(keep != 6)(functools.partial(fetch, inside, k))
        else:
            for case, source in enumerate((direct, crossed)[k >> 1]):
                pl.when(keep == case)(functools.partial(fetch, source, k))


def wait_columns(k, col_buf, sems):
    pltpu.make_async_copy(col_buf.at[k], col_buf.at[k], sems.at[k, 0]).wait()


def tile(stacked, scaled):
    return lax.dot_general(stacked, scaled, (((1,), (1,)), ((), ())), preferred_element_type=jnp.float32)


def stack_columns(columns):
    width = columns.shape[1] // 2
    turned = jnp.concatenate([-columns[:, width:], columns[:, :width]], axis=1)
    return jnp.concatenate([columns, turned], axis=0)


def occ_kernel(cases, *refs):
    direct, crossed = refs[:cases], refs[cases : 2 * cases]
    recv, last, scaled_ref, out_ref, col_buf, sems = refs[2 * cases :]
    load_columns(0, range(4), direct, crossed, recv, last, col_buf, sems)
    per_group = col_buf.shape[1]
    for k in range(4):
        wait_columns(k, col_buf, sems)
        for i in range(per_group):
            stacked = stack_columns(col_buf[k, i])
            for half in range(2):
                out_ref[k * per_group + i, half] = tile(stacked, scaled_ref[half, k, i])


STRIP = 16


def pair_sums(moved, occ_ref, pair_ref, first, before, store):
    per_part, halves = moved[0].shape[:2]
    count = per_part * len(moved)
    block = moved[0].shape[2] // 2
    transfers = pair_ref.shape[0]
    held = [[pair_ref[q, first + a] for a in range(count)] for q in range(transfers)]
    for half in range(halves):

        def strip(index, carry):
            real_rows = pl.ds(pl.multiple_of(index * STRIP, STRIP), STRIP)
            imag_rows = pl.ds(pl.multiple_of(index * STRIP + block, STRIP), STRIP)
            sums = [[None, None] for _ in range(transfers)]
            if before is not None:
                sums = [[before[q, half, comp, real_rows, :] for comp in range(2)] for q in range(transfers)]
            for a in range(count):
                held_part = moved[a // per_part]
                re = held_part[a % per_part, half, real_rows, :]
                im = held_part[a % per_part, half, imag_rows, :]
                for q in range(transfers):
                    ro = occ_ref[held[q][a], half, real_rows, :]
                    io = occ_ref[held[q][a], half, imag_rows, :]
                    for comp, piece in enumerate((ro * re + io * im, io * re - ro * im)):
                        sums[q][comp] = piece if sums[q][comp] is None else sums[q][comp] + piece
            for q in range(transfers):
                for comp in range(2):
                    store(half, real_rows, q, comp, sums[q][comp])
            return carry

        lax.fori_loop(0, block // STRIP, strip, 0)


def scale_kernel(kind, *refs):
    rows, weight_ref, scaled_ref = refs[:8], *refs[8:]
    groups, slots = scaled_ref.shape[1:3]
    group = lax.axis_index("kgrp")
    for k in range(groups):
        for half in range(2):
            panels = rows[half * groups + k]
            skip = panels.shape[0] - slots
            for i in range(slots):
                panel = panels[kind * skip + i].astype(jnp.float32)
                parts = []
                for t in range(weight_ref.shape[1]):
                    weight = weight_ref[kind, t, pl.ds((group ^ k) * slots + i, 1), :]
                    parts.append((panel * weight).astype(jnp.bfloat16))
                scaled_ref[half, k, i] = jnp.concatenate(parts, axis=0)


def emp_tiles_kernel(k, cases, *refs):
    scaled_ref, moved, col_buf, sems = refs[-4:]
    if k:
        load_columns(1, (k,), None, None, refs[0], None, col_buf, sems)
    else:
        load_columns(1, (k,), grouped(refs[:-4], cases), None, None, None, col_buf, sems)
    wait_columns(k, col_buf, sems)
    for i in range(col_buf.shape[1]):
        stacked = stack_columns(col_buf[k, i])
        for half in range(2):
            moved[i, half] = tile(stacked, scaled_ref[half, k, i])


def sums_kernel(own, given, pair_ref, occ_ref, sum_ref):
    def store(half, rows_at, q, comp, value):
        sum_ref[q, half, comp, rows_at, :] = value

    pair_sums((own, given), occ_ref, pair_ref, 0, None, store)


def closing_kernel(factor, cases, *refs):
    crossed = list(refs[: cases - 1]) + [refs[cases - 1 : cases + 1]]
    recv, scaled_ref, pair_ref, occ_ref, sum_ref, out_ref, col_buf, moved, sems = refs[cases + 1 : cases + 2] + refs[cases + 4 :]
    last = refs[cases + 2 : cases + 4]
    load_columns(1, (2, 3), None, crossed, recv, last, col_buf, sems)
    per_group, block = col_buf.shape[1:3]
    times = out_ref.shape[3]
    y = lax.axis_index("col")
    for k in (2, 3):
        wait_columns(k, col_buf, sems)
        for i in range(per_group):
            stacked = stack_columns(col_buf[k, i])
            for half in range(2):
                moved[(k - 2) * per_group + i, half] = tile(stacked, scaled_ref[half, k, i])

    def store(half, rows_at, q, comp, value):
        start = pl.multiple_of((y ^ half) * block, LANES)
        value = value * factor
        for t in range(times):
            out_ref[comp, q, rows_at, t, pl.ds(start, block)] = value[:, t * block : (t + 1) * block]

    pair_sums((moved,), occ_ref, pair_ref, 2 * per_group, sum_ref, store)


def output_stationary(occ_orbitals, emp_orbitals, energies, band_order, imag_times, kq_map, slot_kpoint):
    groups, rows, cols = (lax.axis_size(name) for name in AXES)
    slots, block = occ_orbitals.shape[:2]
    width = occ_orbitals.shape[2] * occ_orbitals.shape[3]
    transfers, times = kq_map.shape[0], imag_times.shape[0]
    kpoints = groups * slots
    half = rows // 2
    top = rows - 1

    def send(array, route):
        pairs = []
        for g in range(groups):
            for z in range(rows):
                for y in range(cols):
                    target = route(g // 2, g % 2, z, y)
                    if target is not None:
                        x2, h2, z2, y2 = target
                        pairs.append(((g * rows + z) * cols + y, ((2 * x2 + h2) * rows + z2) * cols + y2))
        return lax.ppermute(array, AXES, pairs)

    def inner(z):
        return z in (half - 1, half)

    def near(x, z):
        return x == z // half

    def swap(x, h, z, y):
        return x, h, z ^ 1, y

    def swap_main(x, h, z, y):
        return None if inner(z) and near(x, z) else (x, h, z ^ 1, y)

    def swap_late(x, h, z, y):
        return (x, h, z ^ 1, y) if inner(z) and near(x, z) else None

    def middle(x, h, z, y):
        return (x, h, top - z, y) if inner(z) else None

    def outward_near(x, h, z, y):
        return (x, h, z ^ 1, y) if inner(z) and near(x, z) else None

    def outward_far(x, h, z, y):
        return (x, h, z ^ 1, y) if inner(z) and not near(x, z) else None

    def flip_x(x, h, z, y):
        return 1 - x, h, z, y

    def middle_or_to_near(x, h, z, y):
        if inner(z):
            return x, h, top - z, y
        return None if near(x, z) else (1 - x, h, z, y)

    def from_near(x, h, z, y):
        if not near(x, z):
            return None
        return (x, h, top - z, y) if inner(z) else (x, h, z ^ 1, y)

    def inward_near(x, h, z, y):
        return (x, h, z ^ 1, y) if near(x, z) and not inner(z) else None

    def to_far_or_outward(x, h, z, y):
        if not inner(z):
            return None
        return (1 - x, h, z, y) if near(x, z) else (x, h, z ^ 1, y)

    def to_far_outer(x, h, z, y):
        return (1 - x, h, z, y) if near(x, z) and not inner(z) else None

    def to_owner(x, h, z, y):
        owner = h != z // half
        return (1 - x, h, z, y) if near(x, z) and not inner(z) and owner else None

    def to_other_owner(x, h, z, y):
        owner = h != z // half
        return None if owner or inner(z) or not near(x, z) else (1 - x, 1 - h, z, y)

    def outward_owner(x, h, z, y):
        owner = h != z // half
        return (x, h, z ^ 1, y) if inner(z) and not near(x, z) and owner else None

    def outward_other(x, h, z, y):
        owner = h != z // half
        return None if owner or near(x, z) or not inner(z) else (x, 1 - h, z ^ 1, y)

    def to_far_inner(x, h, z, y):
        return (1 - x, h, z, y) if near(x, z) and inner(z) else None

    def flip_y(x, h, z, y):
        return x, h, z, 1 - y

    def flip_core(x, h, z, y):
        return x, 1 - h, z, y

    flat = jax.ShapeDtypeStruct((slots, block, width), jnp.bfloat16)
    occ_flat = pl.pallas_call(
        flatten_occ_kernel,
        out_shape=flat,
        in_specs=[VMEM],
        out_specs=VMEM,
        compiler_params=LIMIT,
        name="flatten_occ",
    )(occ_orbitals)
    single = jax.ShapeDtypeStruct((1, block, width), jnp.bfloat16)
    emp_flat, both, *emp_parts = pl.pallas_call(
        flatten_emp_kernel,
        out_shape=[flat, jax.ShapeDtypeStruct((2 * slots, block, width), jnp.bfloat16)] + [single] * slots,
        in_specs=[VMEM] * 2,
        out_specs=[VMEM] * (2 + slots),
        compiler_params=LIMIT,
        name="flatten_emp",
    )(emp_orbitals, occ_flat)
    kinds = [occ_flat, emp_flat]

    prepare = pl.pallas_call(
        prep_kernel,
        out_shape=[
            jax.ShapeDtypeStruct((2, times, kpoints, width), jnp.float32),
            jax.ShapeDtypeStruct((transfers, kpoints), jnp.int32),
        ],
        in_specs=[HBM, HBM, SMEM, SMEM, SMEM],
        out_specs=[VMEM, SMEM],
        scratch_shapes=[
            pltpu.SMEM((kpoints,), jnp.int32),
            pltpu.VMEM(energies.shape, energies.dtype),
            pltpu.VMEM(band_order.shape, band_order.dtype),
            pltpu.SemaphoreType.DMA((2,)),
        ],
        compiler_params=LIMIT,
        name="prep",
    )
    weights, pairs = prepare(energies, band_order, imag_times, kq_map, slot_kpoint)

    s1 = [send(kinds[0], swap), send(kinds[1], swap_main)]
    late = [send(emp_parts[slot], swap_late) for slot in range(slots)]
    b = [send(kinds[i], middle) for i in range(2)]
    crossed = send(both, flip_x)
    turned = send(both, flip_y)
    sibling = send(both, flip_core)
    d = [send(s1[i], middle_or_to_near) for i in range(2)]
    en = [send(b[i], outward_near) for i in range(2)]
    e = [send(b[0], to_far_or_outward), send(b[1], outward_far)]
    bx = [send(crossed[:slots], inward_near), send(crossed[slots:], from_near)]
    turned_crossed = send(crossed, flip_y)
    crossed_sibling = send(crossed, flip_core)
    turned_sibling = send(turned, flip_core)
    turned_crossed_sibling = send(turned_crossed, flip_core)
    ex = [send(en[i], to_far_outer) for i in range(2)]
    head = slots // 2
    fn = [send(d[0], outward_near), send(d[1][:head], outward_near)]
    f = [send(d[0], to_far_or_outward), send(d[1], outward_far)]
    dx = [f[0], send(d[1], to_far_inner)]
    fx = [send(fn[0], to_owner), send(fn[1], to_owner)]
    rest = dx[1][head:]
    last = [[send(fn[0], to_other_owner)], [send(fn[1], to_other_owner), send(rest, outward_other)]]
    outer_rest = send(rest, outward_owner)
    row_panels, direct, across, given = [], [], [], []
    for kind in range(2):
        row_panels.append([
            kinds[kind], sibling, crossed, crossed_sibling,
            turned, turned_sibling, turned_crossed, turned_crossed_sibling,
        ])
        swapped = late if kind else s1[:1]
        direct.append([kinds[kind], s1[kind], *swapped, b[kind], d[kind], e[kind], f[kind]])
        across.append([crossed, bx[kind], d[kind], bx[1] if kind else e[0], dx[kind], ex[kind], fx[kind]] + [outer_rest] * kind)
        ready = across[kind][:6] + [ex[kind]]
        give = pack(kind, direct[kind], ready, (slots, block, width))
        given.append(send(give, flip_core))

    column_scratch = pltpu.VMEM((4, slots, block, width), jnp.bfloat16)
    cases = len(across[0])
    scaled = []
    for kind in range(2):
        scale = pl.pallas_call(
            functools.partial(scale_kernel, kind),
            out_shape=jax.ShapeDtypeStruct((2, 4, slots, times * block, width), jnp.bfloat16),
            in_specs=[VMEM] * 9,
            out_specs=VMEM,
            compiler_params=pltpu.CompilerParams(vmem_limit_bytes=20 * 2**20),
        )
        scaled.append(scale(*row_panels[kind], weights))
    occ_tiles = pl.pallas_call(
        functools.partial(occ_kernel, cases),
        out_shape=jax.ShapeDtypeStruct((kpoints, 2, 2 * block, times * block), jnp.float32),
        in_specs=[HBM] * (2 + 2 * cases) + [VMEM],
        out_specs=VMEM,
        scratch_shapes=[column_scratch, pltpu.SemaphoreType.DMA((4, 1))],
        compiler_params=LIMIT,
        name="occ_tiles",
    )
    tiles = occ_tiles(*direct[0], *across[0], given[0], *last[0], scaled[0])
    half_tiles = (kpoints // 2, 2, 2 * block, times * block)
    moved = []
    for k, panels in enumerate((direct[1], given[1:])):
        emp_tiles = pl.pallas_call(
            functools.partial(emp_tiles_kernel, k, cases),
            out_shape=jax.ShapeDtypeStruct((slots,) + half_tiles[1:], jnp.float32),
            in_specs=[HBM] * len(panels) + [VMEM],
            out_specs=VMEM,
            scratch_shapes=[column_scratch, pltpu.SemaphoreType.DMA((4, 1))],
            compiler_params=LIMIT,
        )
        moved.append(emp_tiles(*panels, scaled[1]))
    direct_sums = pl.pallas_call(
        sums_kernel,
        out_shape=jax.ShapeDtypeStruct((transfers, 2, 2, block, times * block), jnp.float32),
        in_specs=[VMEM, VMEM, SMEM, VMEM],
        out_specs=VMEM,
        compiler_params=LIMIT,
        name="direct_sums",
    )
    sums = direct_sums(*moved, pairs, tiles)
    result = pl.pallas_call(
        functools.partial(closing_kernel, -1.0 / kpoints, cases),
        out_shape=jax.ShapeDtypeStruct((2, transfers, block, times, cols * block), jnp.float32),
        in_specs=[HBM] * (4 + cases) + [VMEM, SMEM, VMEM, VMEM],
        out_specs=VMEM,
        scratch_shapes=[column_scratch, pltpu.VMEM(half_tiles, jnp.float32), pltpu.SemaphoreType.DMA((4, 1))],
        compiler_params=LIMIT,
        name="closing",
    )(*across[1], given[1], *last[1], scaled[1], pairs, tiles, sums)
    return result[:, :, None]


def staged(*arguments):
    return output_stationary(*arguments)


def solution(mesh):
    in_specs = (
        P("kgrp", ("row", "col"), None, None),
        P("kgrp", ("row", "col"), None, None),
        P(),
        P(),
        P(),
        P(),
        P(),
    )
    out_specs = P(None, None, "col", "kgrp", None, "row")
    groups, rows, cols = (mesh.shape[name] for name in AXES)
    line = groups == rows == 2 * cols == 4
    body = staged if line else summed_over_groups
    return jax.shard_map(body, mesh=mesh, in_specs=in_specs, out_specs=out_specs, check_vma=False)
```
